512 devices in a mesh: face: 128 (over y_hi, z, x), chan: 4 (over y_lo, core).
Axes of the slice: x: 4, y: 8 (y_hi: 4, y_lo: 2; y = y_hi * 2 + y_lo), z: 8, core: 2. Of those that a mesh axis runs over, the one named last changes fastest.
Arguments:
- field_in: bfloat16 [256, 131072], P('chan', 'face'), may hold values from -6 to 6
- edge_codes: int32 [128, 4], replicated, may hold values from 0 to 7
- weight_enc: bfloat16 [9, 256, 256], P(None, 'chan'), may hold values from -0.125 to 0.125
- bias_enc: float32 [256], P('chan'), may hold values from -3 to 3
- weight_mid_a: bfloat16 [9, 256, 256], P(None, 'chan'), may hold values from -0.125 to 0.125
- bias_mid_a: float32 [256], P('chan'), may hold values from -3 to 3
- weight_mid_b: bfloat16 [9, 256, 256], P(None, 'chan'), may hold values from -0.125 to 0.125
- bias_mid_b: float32 [256], P('chan'), may hold values from -3 to 3
- weight_dec: bfloat16 [9, 256, 256], P(None, 'chan'), may hold values from -0.125 to 0.125
- bias_dec: float32 [256], P('chan'), may hold values from -3 to 3
Outputs:
- field_out: bfloat16 [256, 131072], P('chan', 'face')
The draws below stay inside these ranges and needn't reach their ends.
Inputs may be any that keep to these rules, and one draw needn't show every extreme that they name: edge_codes[t, s] mod 4 names the edge (0 top row, 1 bottom row, 2 left column, 3 right column) of tile t's neighbour on side s that borders it; a value of 4 or more means that edge is read in reverse order.
All inputs are finite; a program needn't handle non-finite values.
Results may differ from the reference program's by a relative error of at most 0.012.
Values may be sent and summed in bfloat16 or wider, within the bound.
A program may use at most 64 MiB of HBM per device.

```python
import jax
import jax.numpy as jnp

C = 256
B = 32
TILE_COLS = 4
TILES = 128


def with_ends(drawn, stream_key, low, top_value):
    place = [jax.random.randint(jax.random.fold_in(stream_key, axis), (), 0, length) for axis, length in enumerate(drawn.shape)]
    main_axis = drawn.shape.index(max(drawn.shape))
    beside = place[:main_axis] + [(place[main_axis] + 1) % drawn.shape[main_axis]] + place[main_axis + 1:]
    return drawn.at[tuple(place)].set(low).at[tuple(beside)].set(top_value)


def shard_levels(stream_key, dims, cuts, least, high):
    factor_of, own = 1.0, jax.random.fold_in(stream_key, 6)
    for dim, parts in cuts:
        steps = jnp.exp(jax.random.uniform(jax.random.fold_in(own, dim), (parts,), jnp.float32, least / len(cuts), high / len(cuts)))
        factor_of = factor_of * jnp.repeat(steps, dims[dim] // parts).reshape([-1 if axis == dim else 1 for axis in range(len(dims))])
    return factor_of


def normal_values(own_key, shape, width, reach, shards=(), kind=jnp.bfloat16):
    array = jax.random.normal(own_key, shape, jnp.float32) * width
    if len(shards) > 0:
        array = shard_levels(own_key, shape, shards, -0.22, 0.18) * array
    return jnp.clip(array, min=-reach, max=reach).astype(kind)


def setup_inputs(seed: int = 0) -> dict:
    seeds = jax.random.split(jax.random.key(seed), 11)
    return {
        "field_in": normal_values(seeds[0], (C, TILES * B * B), 1.0, 6.0, ((0, 4), (1, 128))),
        "edge_codes": with_ends(jax.random.randint(seeds[1], (TILES, 4), 0, 8), jax.random.fold_in(seeds[1], 1), 0, 7).astype(jnp.int32),
        "weight_enc": normal_values(seeds[2], (9, C, C), (9 * C) ** -0.5, 0.125, ((1, 4),)),
        "bias_enc": normal_values(seeds[3], (C,), 0.5, 3.0, ((0, 4),), jnp.float32),
        "weight_mid_a": normal_values(seeds[4], (9, C, C), (9 * C) ** -0.5, 0.125, ((1, 4),)),
        "bias_mid_a": normal_values(seeds[5], (C,), 0.5, 3.0, ((0, 4),), jnp.float32),
        "weight_mid_b": normal_values(seeds[6], (9, C, C), (9 * C) ** -0.5, 0.125, ((1, 4),)),
        "bias_mid_b": normal_values(seeds[7], (C,), 0.5, 3.0, ((0, 4),), jnp.float32),
        "weight_dec": normal_values(seeds[8], (9, C, C), (9 * C) ** -0.5, 0.125, ((1, 4),)),
        "bias_dec": normal_values(seeds[9], (C,), 0.5, 3.0, ((0, 4),), jnp.float32),
    }


def gather_rims(fields, edge_codes):
    extent = fields.shape[-1]
    tile_count = fields.shape[1]
    border_rows = jnp.stack([fields[:, :, 0, :], fields[:, :, extent - 1, :], fields[:, :, :, 0], fields[:, :, :, extent - 1]], axis=0)
    tile_ids = jnp.arange(tile_count, dtype=jnp.int32)
    offsets = (-TILE_COLS, TILE_COLS, -1, 1)
    rim_list = []
    for side_index in range(4):
        neighbour = (tile_ids + offsets[side_index]) % tile_count
        edge_code = edge_codes[:, side_index]
        picked = border_rows[edge_code % 4, :, neighbour, :]
        picked = jnp.where((edge_code >= 4)[:, None, None], picked[:, :, ::-1], picked)
        rim_list.append(jnp.transpose(picked, (1, 0, 2)))
    north_rim, south_rim, west_rim, east_rim = rim_list
    middle = jnp.concatenate([west_rim[:, :, :, None], fields, east_rim[:, :, :, None]], axis=3)
    top_row = jnp.pad(north_rim, ((0, 0), (0, 0), (1, 1)))[:, :, None, :]
    bottom = jnp.pad(south_rim, ((0, 0), (0, 0), (1, 1)))[:, :, None, :]
    return jnp.concatenate([top_row, middle, bottom], axis=2)


def convolve(padded, weights):
    channels, tile_count, padded_width, _ = padded.shape
    extent = padded_width - 2
    stride = padded_width * padded_width + 2
    flattened = jnp.pad(padded.reshape(channels, tile_count, padded_width * padded_width), ((0, 0), (0, 0), (0, 2)))
    flattened = flattened.reshape(channels, tile_count * stride)
    out_length = tile_count * stride - 2 * padded_width - 2
    running = jnp.zeros((weights.shape[1], out_length), jnp.float32)
    for kernel_tap in range(9):
        offset = (kernel_tap // 3) * padded_width + kernel_tap % 3
        running = running + jnp.dot(weights[kernel_tap], flattened[:, offset:offset + out_length], preferred_element_type=jnp.float32)
    running = jnp.pad(running, ((0, 0), (0, tile_count * stride - out_length)))
    running = running.reshape(-1, tile_count, stride)[:, :, :extent * padded_width]
    running = running.reshape(-1, tile_count, extent, padded_width)
    return running[:, :, :, :extent]


def conv_block(fields, edge_codes, weights, bias_vec):
    convolved = convolve(gather_rims(fields, edge_codes), weights) + bias_vec[:, None, None, None]
    return (fields.astype(jnp.float32) + jax.nn.gelu(convolved, approximate=True)).astype(jnp.bfloat16)


def reference(field_in, edge_codes, weight_enc, bias_enc, weight_mid_a, bias_mid_a, weight_mid_b, bias_mid_b, weight_dec, bias_dec):
    fields = field_in.reshape(C, TILES, B, B)
    encoded = conv_block(fields, edge_codes, weight_enc, bias_enc)
    half_side = B // 2
    coarse = encoded.astype(jnp.float32).reshape(C, TILES, half_side, 2, half_side, 2).mean(axis=(3, 5)).astype(jnp.bfloat16)
    middle_a = conv_block(coarse, edge_codes, weight_mid_a, bias_mid_a)
    middle_b = conv_block(middle_a, edge_codes, weight_mid_b, bias_mid_b)
    refined = jnp.repeat(jnp.repeat(middle_b, 2, axis=2), 2, axis=3)
    joined = (refined.astype(jnp.float32) + encoded.astype(jnp.float32)).astype(jnp.bfloat16)
    result = conv_block(joined, edge_codes, weight_dec, bias_dec)
    return result.reshape(C, TILES * B * B)
```

```python
import functools

import jax
import jax.numpy as jnp
from jax import lax
from jax.experimental import pallas as pl
from jax.experimental.pallas import tpu as pltpu
from jax.sharding import PartitionSpec as P

TILE_COLS = 4
CB = 64
PEERS = 4
C = CB * PEERS
S1 = 32
S2 = 16
Q = 4
QW = S1 * S1 // Q
GELU_A = 0.7978845608028654
GELU_B = 0.044715
MESH = pl.DeviceIdType.MESH
F32 = jnp.float32
BF16 = jnp.bfloat16


def iota(shape, dim):
    return lax.broadcasted_iota(jnp.int32, shape, dim)


def gelu(v):
    return 0.5 * v * (1.0 + jnp.tanh(GELU_A * (v + GELU_B * (v * v * v))))


def dot(a, b):
    return lax.dot_general(a, b, (((1,), (0,)), ((), ())), preferred_element_type=F32)


def dot_t(a, b):
    return lax.dot_general(a, b, (((1,), (1,)), ((), ())), preferred_element_type=F32)


def one_hot(cond):
    return jnp.where(cond, 1.0, 0.0).astype(BF16)


def edge_position(edge, along, side):
    return jnp.where(
        edge == 0,
        along,
        jnp.where(
            edge == 1,
            (side - 1) * side + along,
            jnp.where(edge == 2, along * side, along * side + side - 1),
        ),
    )


def kernel(
    tiles,
    codes,
    x_hbm,
    w0_hbm,
    w1_hbm,
    w2_hbm,
    w3_hbm,
    b0_hbm,
    b1_hbm,
    b2_hbm,
    b3_hbm,
    out_ref,
    g1,
    g2,
    g3,
    g4,
    enc,
    w_v,
    b_v,
    bias_v,
    sel1,
    sel2,
    exp1,
    exp2,
    pool,
    sb,
    rb,
    taps,
    x_sem,
    w_sem,
    b_sem,
    fine_send,
    fine_recv,
    coarse_send,
    coarse_recv,
    rim_send,
    rim_recv,
):
    tile = lax.axis_index("face")
    chan = lax.axis_index("chan")
    partner = chan + 1 - 2 * (chan % 2)
    across = (chan + 2) % 4
    diagonal = (partner + 2) % 4
    near = [
        (tile + TILE_COLS) % tiles,
        (tile + tiles - TILE_COLS) % tiles,
        (tile + 1) % tiles,
        (tile + tiles - 1) % tiles,
    ]
    mine = pl.ds(pl.multiple_of(chan * CB, CB), CB)
    across_rows = pl.ds(pl.multiple_of(across * CB, CB), CB)

    x_copies = [
        pltpu.make_async_copy(x_hbm.at[:, pl.ds(q * QW, QW)], g1.at[q, mine, :], x_sem.at[q])
        for q in range(Q)
    ]
    for copy in x_copies:
        copy.start()
    w_copies = []
    b_copies = []
    for i, w in enumerate((w0_hbm, w1_hbm, w2_hbm, w3_hbm)):
        w_copies.append(pltpu.make_async_copy(w, w_v.at[i], w_sem.at[i]))
    for i, b in enumerate((b0_hbm, b1_hbm, b2_hbm, b3_hbm)):
        b_copies.append(pltpu.make_async_copy(b, b_v.at[i], b_sem.at[i]))
    for copy in w_copies + b_copies:
        copy.start()

    barrier = pltpu.get_barrier_semaphore()
    for peer in (partner, across, diagonal):
        pl.semaphore_signal(barrier, inc=1, device_id=(tile, peer), device_id_type=MESH)
    for side in range(4):
        for step in range(PEERS):
            peer = (chan + step) % PEERS
            pl.semaphore_signal(
                barrier, inc=1, device_id=(near[side], peer), device_id_type=MESH
            )

    lane = iota((1, 128), 1)
    slot = lane // 32
    along = lane % 32
    codes_here = [codes[side, near[side]] for side in range(4)]
    code = jnp.where(
        slot == 0,
        codes_here[0],
        jnp.where(slot == 1, codes_here[1], jnp.where(slot == 2, codes_here[2], codes_here[3])),
    )
    edge = code % 4
    for size, sel in ((S1, sel1), (S2, sel2)):
        place = jnp.where(code >= 4, size - 1 - along, along)
        cell = jnp.where(along < size, edge_position(edge, place, size), -1)
        sel[...] = one_hot(iota((size * size, 128), 0) == cell)
    row = iota((128, 1), 0)
    for size, exp in ((S1, exp1), (S2, exp2)):
        cell = jnp.where(
            row % 32 < size, edge_position(row // 32, row % 32, size), -1
        )
        exp[...] = one_hot(iota((128, size * size), 1) == cell)
    cell = iota((QW, QW), 0)
    pool[...] = one_hot(
        (cell // S1 // 2) * S2 + (cell % S1) // 2 == iota((QW, QW), 1) % (QW // 4)
    )
    eye = iota((CB, CB), 0) == iota((CB, CB), 1)
    for copy in b_copies:
        copy.wait()
    for i in range(4):
        column = jnp.sum(
            jnp.where(eye, jnp.broadcast_to(b_v[i], (CB, CB)), 0.0), axis=1, keepdims=True
        )
        bias_v[i] = jnp.broadcast_to(column, (CB, 128))

    def pack_rims(layer, picked):
        for side in range(4):
            block = None
            for group in range(4):
                part = picked[16 * group : 16 * group + 16, :]
                shift = (32 * (group - side)) % 128
                if shift:
                    part = pltpu.roll(part, shift, 1)
                block = part if block is None else jnp.where(slot == group, part, block)
            sb[layer, side] = block.astype(BF16)

    def rim_copies(layer):
        copies = []
        for step in range(PEERS):
            for side in range(4):
                peer = (chan + step) % PEERS
                copies.append(
                    pltpu.make_async_remote_copy(
                        src_ref=sb.at[layer, side],
                        dst_ref=rb.at[layer, chan, side],
                        send_sem=rim_send.at[layer, step, side],
                        recv_sem=rim_recv.at[layer, step, side],
                        device_id=(near[side], peer),
                        device_id_type=MESH,
                    )
                )
        return copies

    def fine_copies(index, g):
        def copies_to(kind, peer, rows):
            return [
                pltpu.make_async_remote_copy(
                    src_ref=g.at[q, rows, :],
                    dst_ref=g.at[q, rows, :],
                    send_sem=fine_send.at[index, kind, q],
                    recv_sem=fine_recv.at[index, kind, q],
                    device_id=(tile, peer),
                    device_id_type=MESH,
                )
                for q in range(Q)
            ]

        return (
            copies_to(0, partner, mine),
            copies_to(1, across, mine),
            copies_to(2, partner, across_rows),
        )

    def coarse_copies(index, g):
        return [
            pltpu.make_async_remote_copy(
                src_ref=g.at[mine, :],
                dst_ref=g.at[mine, :],
                send_sem=coarse_send.at[index, kind],
                recv_sem=coarse_recv.at[index, kind],
                device_id=(tile, peer),
                device_id_type=MESH,
            )
            for kind, peer in enumerate((across, diagonal, partner))
        ]

    def rim_sums(layer, size, exp):
        blocks = []
        for source in range(PEERS):
            parts = [rb[layer, source, side].astype(F32) for side in range(4)]
            for group in range(4):
                block = None
                for side in range(4):
                    part = parts[side]
                    shift = (32 * (side - group)) % 128
                    if shift:
                        part = pltpu.roll(part, shift, 1)
                    block = part if block is None else jnp.where(slot == side, part, block)
                blocks.append(block.astype(BF16))
        rims = jnp.concatenate(blocks, axis=0)
        r = dot(w_v[layer].reshape(9 * CB, C), rims)
        r = [r[CB * t : CB * t + CB, :] for t in range(9)]

        def by_side(north, south, west, east):
            return jnp.where(
                slot == 0,
                r[north],
                jnp.where(slot == 1, r[south], jnp.where(slot == 2, r[west], r[east])),
            )

        before = jnp.where(along == 0, 0.0, pltpu.roll(by_side(0, 6, 0, 2), 1, 1))
        after = jnp.where(along == size - 1, 0.0, pltpu.roll(by_side(2, 8, 6, 8), 127, 1))
        total = before + by_side(1, 7, 3, 5) + after
        high = total.astype(BF16)
        low = (total - high.astype(F32)).astype(BF16)
        spread = dot(jnp.concatenate([high, low], axis=0), exp[...])
        return spread[:CB] + spread[CB:]

    def conv_rows(layer, size, rows, rims):
        cells = size * size
        place = iota((1, cells), 1)
        column = place % size
        sums = []
        for dx in range(3):
            t = [taps[pl.ds(CB * (3 * dy + dx) + rows, 16), :cells] for dy in range(3)]
            above = jnp.where(place >= size, pltpu.roll(t[0], size, 1), 0.0)
            below = jnp.where(place < cells - size, pltpu.roll(t[2], cells - size, 1), 0.0)
            sums.append(t[1] + (above + below))
        left = jnp.where(column == 0, 0.0, pltpu.roll(sums[0], 1, 1))
        right = jnp.where(column == size - 1, 0.0, pltpu.roll(sums[2], cells - 1, 1))
        bias = bias_v[layer, rows : rows + 16, 0:1]
        return (sums[1] + (left + right)) + (rims[rows : rows + 16, :] + bias)

    for copy in x_copies:
        copy.wait()
    picked = sum(dot(g1[q, mine, :], sel1[QW * q : QW * q + QW, :]) for q in range(Q))
    pack_rims(0, picked)

    pl.semaphore_wait(barrier, 3 + 4 * PEERS)

    sent = []
    rims0 = rim_copies(0)
    to_partner, to_across, relay = fine_copies(0, g1)
    for q in range(Q):
        to_across[q].start()
    for copy in rims0:
        copy.start()
    for q in range(Q):
        to_partner[q].start()
    for q in range(Q):
        to_across[q].wait_recv()
        relay[q].start()
    w_copies[0].wait()
    for q in range(Q):
        to_partner[q].wait_recv()
        relay[q].wait_recv()
        taps[:, QW * q : QW * q + QW] = dot(w_v[0].reshape(9 * CB, C), g1[q])
    for copy in rims0:
        copy.wait_recv()
    sent += rims0 + to_partner + to_across + relay
    rims = rim_sums(0, S1, exp1)
    for rows in range(0, CB, 16):
        act = gelu(conv_rows(0, S1, rows, rims))
        own = pl.ds(pl.multiple_of(chan * CB + rows, 16), 16)
        for q in range(Q):
            field = g1[q, own, :].astype(F32)
            enc[q, rows : rows + 16, :] = (field + act[:, QW * q : QW * q + QW]).astype(BF16)

    group = iota((1, QW), 1) // (QW // 4)
    pooled = dot(enc[...].reshape(Q * CB, QW), pool[...])
    coarse = pooled[:CB]
    for q in range(1, Q):
        coarse = jnp.where(group == q, pooled[CB * q : CB * q + CB], coarse)
    coarse = (coarse * 0.25).astype(BF16)
    middle = coarse
    for layer, g in ((1, g2), (2, g3)):
        g[mine, :] = middle
        pack_rims(layer, dot(middle, sel2[...]))
        rims_l = rim_copies(layer)
        copies = coarse_copies(layer - 1, g)
        for copy in rims_l:
            copy.start()
        for copy in copies:
            copy.start()
        w_copies[layer].wait()
        for copy in copies:
            copy.wait_recv()
        taps[:, :QW] = dot(w_v[layer].reshape(9 * CB, C), g[...])
        for copy in rims_l:
            copy.wait_recv()
        sent += rims_l + copies
        rims = rim_sums(layer, S2, exp2)
        parts = []
        for rows in range(0, CB, 16):
            act = gelu(conv_rows(layer, S2, rows, rims))
            parts.append((middle[rows : rows + 16, :].astype(F32) + act).astype(BF16))
        middle = jnp.concatenate(parts, axis=0)

    spread = jnp.concatenate(
        [jnp.where(group == q, middle.astype(F32), 0.0).astype(BF16) for q in range(Q)], axis=0
    )
    refined = dot_t(spread, pool[...])
    picked = None
    for q in range(Q):
        joined = (refined[CB * q : CB * q + CB] + enc[q].astype(F32)).astype(BF16)
        g4[q, mine, :] = joined
        part = dot(joined, sel1[QW * q : QW * q + QW, :])
        picked = part if picked is None else picked + part
    pack_rims(3, picked)
    rims3 = rim_copies(3)
    to_partner, to_across, relay = fine_copies(1, g4)
    for copy in rims3:
        copy.start()
    for q in range(Q):
        to_across[q].start()
    for q in range(Q):
        to_partner[q].start()
    for q in range(Q):
        to_across[q].wait_recv()
        relay[q].start()
    w_copies[3].wait()
    for q in range(Q):
        to_partner[q].wait_recv()
        relay[q].wait_recv()
        taps[:, QW * q : QW * q + QW] = dot(w_v[3].reshape(9 * CB, C), g4[q])
    for copy in rims3:
        copy.wait_recv()
    sent += rims3 + to_partner + to_across + relay
    rims = rim_sums(3, S1, exp1)
    for rows in range(0, CB, 16):
        act = gelu(conv_rows(3, S1, rows, rims))
        own = pl.ds(pl.multiple_of(chan * CB + rows, 16), 16)
        for q in range(Q):
            field = g4[q, own, :].astype(F32)
            out_ref[rows : rows + 16, QW * q : QW * q + QW] = (
                field + act[:, QW * q : QW * q + QW]
            ).astype(BF16)
    for copy in sent:
        copy.wait_send()


def on_device(
    tiles,
    field_in,
    edge_codes,
    weight_enc,
    bias_enc,
    weight_mid_a,
    bias_mid_a,
    weight_mid_b,
    bias_mid_b,
    weight_dec,
    bias_dec,
):
    hbm = pl.BlockSpec(memory_space=pltpu.MemorySpace.HBM)
    vmem = pl.BlockSpec(memory_space=pltpu.MemorySpace.VMEM)
    dma = pltpu.SemaphoreType.DMA
    biases = [b.reshape(1, CB) for b in (bias_enc, bias_mid_a, bias_mid_b, bias_dec)]
    return pl.pallas_call(
        functools.partial(kernel, tiles),
        out_shape=jax.ShapeDtypeStruct((CB, S1 * S1), BF16),
        in_specs=[pl.BlockSpec(memory_space=pltpu.MemorySpace.SMEM)] + [hbm] * 9,
        out_specs=vmem,
        scratch_shapes=[
            pltpu.VMEM((Q, C, QW), BF16),
            pltpu.VMEM((C, QW), BF16),
            pltpu.VMEM((C, QW), BF16),
            pltpu.VMEM((Q, C, QW), BF16),
            pltpu.VMEM((Q, CB, QW), BF16),
            pltpu.VMEM((4, 9, CB, C), BF16),
            pltpu.VMEM((4, 1, CB), F32),
            pltpu.VMEM((4, CB, 128), F32),
            pltpu.VMEM((S1 * S1, 128), BF16),
            pltpu.VMEM((S2 * S2, 128), BF16),
            pltpu.VMEM((128, S1 * S1), BF16),
            pltpu.VMEM((128, S2 * S2), BF16),
            pltpu.VMEM((QW, QW), BF16),
            pltpu.VMEM((4, 4, 16, 128), BF16),
            pltpu.VMEM((4, PEERS, 4, 16, 128), BF16),
            pltpu.VMEM((9 * CB, S1 * S1), F32),
            dma((Q,)),
            dma((4,)),
            dma((4,)),
            dma((2, 3, Q)),
            dma((2, 3, Q)),
            dma((2, 3)),
            dma((2, 3)),
            dma((4, PEERS, 4)),
            dma((4, PEERS, 4)),
        ],
        compiler_params=pltpu.CompilerParams(
            collective_id=0, has_side_effects=True, vmem_limit_bytes=62 * 1024 * 1024
        ),
        name="unet_window",
    )(
        edge_codes.T,
        field_in,
        weight_enc,
        weight_mid_a,
        weight_mid_b,
        weight_dec,
        *biases,
    )


def solution(mesh):
    weights = P(None, "chan", None)
    in_specs = (
        P("chan", "face"),
        P(),
        weights,
        P("chan"),
        weights,
        P("chan"),
        weights,
        P("chan"),
        weights,
        P("chan"),
    )
    return jax.shard_map(
        functools.partial(on_device, mesh.shape["face"]),
        mesh=mesh,
        in_specs=in_specs,
        out_specs=P("chan", "face"),
        check_vma=False,
    )
```

```python
import functools

import jax
import jax.numpy as jnp
from jax import lax
from jax.experimental import pallas as pl
from jax.experimental.pallas import tpu as pltpu
from jax.sharding import PartitionSpec as P

TILE_COLS = 4
CB = 64
PEERS = 4
C = CB * PEERS
S1 = 32
S2 = 16
Q = 4
QW = S1 * S1 // Q
GELU_A = 0.7978845608028654
GELU_B = 0.044715
MESH = pl.DeviceIdType.MESH
F32 = jnp.float32
BF16 = jnp.bfloat16


def iota(shape, dim):
    return lax.broadcasted_iota(jnp.int32, shape, dim)


def gelu(v):
    return 0.5 * v * (1.0 + jnp.tanh(GELU_A * (v + GELU_B * (v * v * v))))


def dot(a, b):
    return lax.dot_general(a, b, (((1,), (0,)), ((), ())), preferred_element_type=F32)


def dot_t(a, b):
    return lax.dot_general(a, b, (((1,), (1,)), ((), ())), preferred_element_type=F32)


def one_hot(cond):
    return jnp.where(cond, 1.0, 0.0).astype(BF16)


def edge_position(edge, along, side):
    return jnp.where(
        edge == 0,
        along,
        jnp.where(
            edge == 1,
            (side - 1) * side + along,
            jnp.where(edge == 2, along * side, along * side + side - 1),
        ),
    )


def kernel(
    tiles,
    codes_hbm,
    x_hbm,
    w0_hbm,
    w1_hbm,
    w2_hbm,
    w3_hbm,
    b0_hbm,
    b1_hbm,
    b2_hbm,
    b3_hbm,
    out_ref,
    codes,
    g1,
    g2,
    g3,
    g4,
    g5,
    joined,
    w_v,
    b_v,
    bias_v,
    sel1,
    sel2,
    exp1,
    exp2,
    pool,
    up,
    sb,
    rb,
    taps,
    codes_sem,
    x_sem,
    w_sem,
    b_sem,
    fine_send,
    partner_recv,
    fine_recv,
    coarse_send,
    coarse_recv,
    rim_send,
    rim_recv,
):
    tile = lax.axis_index("face")
    chan = lax.axis_index("chan")
    partner = chan + 1 - 2 * (chan % 2)
    across = (chan + 2) % 4
    diagonal = (partner + 2) % 4
    near = [
        (tile + TILE_COLS) % tiles,
        (tile + tiles - TILE_COLS) % tiles,
        (tile + 1) % tiles,
        (tile + tiles - 1) % tiles,
    ]
    mine = pl.ds(pl.multiple_of(chan * CB, CB), CB)
    across_rows = pl.ds(pl.multiple_of(across * CB, CB), CB)

    barrier = pltpu.get_barrier_semaphore()
    for peer in (partner, across, diagonal):
        pl.semaphore_signal(barrier, inc=1, device_id=(tile, peer), device_id_type=MESH)
    for side in range(4):
        for step in range(PEERS):
            peer = (chan + step) % PEERS
            pl.semaphore_signal(
                barrier, inc=1, device_id=(near[side], peer), device_id_type=MESH
            )

    codes_copy = pltpu.make_async_copy(codes_hbm, codes, codes_sem)
    codes_copy.start()
    x_copies = [
        pltpu.make_async_copy(x_hbm.at[:, pl.ds(q * QW, QW)], g1.at[q, mine, :], x_sem)
        for q in range(Q)
    ]
    for copy in x_copies:
        copy.start()
    w_copies = []
    b_copies = []
    for i, w in enumerate((w0_hbm, w1_hbm, w2_hbm, w3_hbm)):
        w_copies.append(pltpu.make_async_copy(w, w_v.at[i], w_sem.at[i]))
    for i, b in enumerate((b0_hbm, b1_hbm, b2_hbm, b3_hbm)):
        b_copies.append(pltpu.make_async_copy(b, b_v.at[i], b_sem.at[i]))

    lane = iota((1, 128), 1)
    slot = lane // 32
    along = lane % 32

    def wait_bytes(ref, sem):
        pltpu.make_async_copy(ref, ref, sem).wait()

    def pick_table(code, size, sel):
        place = jnp.where(code >= 4, size - 1 - along, along)
        cell = jnp.where(along < size, edge_position(code % 4, place, size), -1)
        sel[...] = one_hot(iota((size * size, 128), 0) == cell)

    def other_tables():
        row = iota((128, 1), 0)
        for size, exp in ((S1, exp1), (S2, exp2)):
            cell = jnp.where(
                row % 32 < size, edge_position(row // 32, row % 32, size), -1
            )
            exp[...] = one_hot(iota((128, size * size), 1) == cell)
        cell = iota((QW, QW), 0)
        pool[...] = one_hot(
            (cell // S1 // 2) * S2 + (cell % S1) // 2 == iota((QW, QW), 1) % (QW // 4)
        )
        cell = iota((1, QW), 1)
        cell = (cell // S1 // 2) * S2 + (cell % S1) // 2
        for q in range(Q):
            up[q] = one_hot(iota((QW, QW), 0) == cell + q * (QW // 4))
        eye = iota((CB, CB), 0) == iota((CB, CB), 1)
        for copy in b_copies:
            copy.wait()
        for i in range(4):
            column = jnp.sum(
                jnp.where(eye, jnp.broadcast_to(b_v[i], (CB, CB)), 0.0), axis=1, keepdims=True
            )
            bias_v[i] = jnp.broadcast_to(column, (CB, 128))

    def pack_rims(layer, picked):
        for side in range(4):
            block = None
            for group in range(4):
                part = picked[16 * group : 16 * group + 16, :]
                shift = (32 * (group - side)) % 128
                if shift:
                    part = pltpu.roll(part, shift, 1)
                block = part if block is None else jnp.where(slot == group, part, block)
            sb[layer, side] = block.astype(BF16)

    def rim_copies(layer):
        copies = []
        for step in range(PEERS):
            for side in range(4):
                peer = (chan + step) % PEERS
                copies.append(
                    pltpu.make_async_remote_copy(
                        src_ref=sb.at[layer, side],
                        dst_ref=rb.at[layer, chan, side],
                        send_sem=rim_send.at[layer],
                        recv_sem=rim_recv.at[layer],
                        device_id=(near[side], peer),
                        device_id_type=MESH,
                    )
                )
        return copies

    def fine_copies(index, g, source):
        def copies_to(kind, peer, rows, source, recv):
            return [
                pltpu.make_async_remote_copy(
                    src_ref=source(q),
                    dst_ref=g.at[q, rows, :],
                    send_sem=fine_send.at[index, kind],
                    recv_sem=recv[q],
                    device_id=(tile, peer),
                    device_id_type=MESH,
                )
                for q in range(Q)
            ]

        return (
            copies_to(0, partner, mine, source, [partner_recv.at[index]] * Q),
            copies_to(1, across, mine, source, [fine_recv.at[index, 0, q] for q in range(Q)]),
            copies_to(
                2,
                partner,
                across_rows,
                lambda q: g.at[q, across_rows, :],
                [fine_recv.at[index, 1, q] for q in range(Q)],
            ),
        )

    def coarse_copies(index, g):
        return [
            pltpu.make_async_remote_copy(
                src_ref=g.at[mine, :],
                dst_ref=g.at[mine, :],
                send_sem=coarse_send.at[index],
                recv_sem=coarse_recv.at[index],
                device_id=(tile, peer),
                device_id_type=MESH,
            )
            for peer in (across, diagonal, partner)
        ]

    def coarse_wait(g, sem):
        wait_bytes(g.at[pl.ds(0, 3 * CB), :], sem)

    def rim_sums(layer, size, exp):
        blocks = []
        for source in range(PEERS):
            parts = [rb[layer, source, side].astype(F32) for side in range(4)]
            for group in range(4):
                block = None
                for side in range(4):
                    part = parts[side]
                    shift = (32 * (side - group)) % 128
                    if shift:
                        part = pltpu.roll(part, shift, 1)
                    block = part if block is None else jnp.where(slot == side, part, block)
                blocks.append(block.astype(BF16))
        rims = jnp.concatenate(blocks, axis=0)
        r = dot(w_v[layer].reshape(9 * CB, C), rims)
        r = [r[CB * t : CB * t + CB, :] for t in range(9)]

        def by_side(north, south, west, east):
            return jnp.where(
                slot == 0,
                r[north],
                jnp.where(slot == 1, r[south], jnp.where(slot == 2, r[west], r[east])),
            )

        before = jnp.where(along == 0, 0.0, pltpu.roll(by_side(0, 6, 0, 2), 1, 1))
        after = jnp.where(along == size - 1, 0.0, pltpu.roll(by_side(2, 8, 6, 8), 127, 1))
        total = before + by_side(1, 7, 3, 5) + after
        high = total.astype(BF16)
        low = (total - high.astype(F32)).astype(BF16)
        spread = dot(jnp.concatenate([high, low], axis=0), exp[...])
        return spread[:CB] + spread[CB:]

    def conv_rows(layer, size, rows, rims):
        cells = size * size
        place = iota((1, cells), 1)
        column = place % size
        sums = []
        for dx in range(3):
            t = [taps[pl.ds(CB * (3 * dy + dx) + rows, 16), :cells] for dy in range(3)]
            above = jnp.where(place >= size, pltpu.roll(t[0], size, 1), 0.0)
            below = jnp.where(place < cells - size, pltpu.roll(t[2], cells - size, 1), 0.0)
            sums.append(t[1] + (above + below))
        left = jnp.where(column == 0, 0.0, pltpu.roll(sums[0], 1, 1))
        right = jnp.where(column == size - 1, 0.0, pltpu.roll(sums[2], cells - 1, 1))
        bias = bias_v[layer, rows : rows + 16, 0:1]
        return (sums[1] + (left + right)) + (rims[rows : rows + 16, :] + bias)

    to_partner, to_across, relay = fine_copies(0, g1, lambda q: x_hbm.at[:, pl.ds(q * QW, QW)])
    pl.semaphore_wait(barrier, 3 + 4 * PEERS)
    for copy in to_across + to_partner:
        copy.start()
    for copy in b_copies + w_copies:
        copy.start()
    codes_copy.wait()
    codes_here = [codes[side, near[side]] for side in range(4)]
    code = jnp.where(
        slot == 0,
        codes_here[0],
        jnp.where(slot == 1, codes_here[1], jnp.where(slot == 2, codes_here[2], codes_here[3])),
    )
    pick_table(code, S1, sel1)
    wait_bytes(g1.at[:, mine, :], x_sem)
    picked = sum(dot(g1[q, mine, :], sel1[QW * q : QW * q + QW, :]) for q in range(Q))
    pack_rims(0, picked)
    for copy in rim_copies(0):
        copy.start()
    pick_table(code, S2, sel2)
    other_tables()
    w_copies[0].wait()
    for q in range(Q):
        to_across[q].wait_recv()
        relay[q].start()
    wait_bytes(g1.at[:, mine, :], partner_recv.at[0])
    for q in range(Q):
        relay[q].wait_recv()
        taps[:, QW * q : QW * q + QW] = dot(w_v[0].reshape(9 * CB, C), g1[q])
    wait_bytes(rb.at[0], rim_recv.at[0])
    rims = rim_sums(0, S1, exp1)
    for rows in range(0, CB, 16):
        act = gelu(conv_rows(0, S1, rows, rims))
        own = pl.ds(pl.multiple_of(chan * CB + rows, 16), 16)
        for q in range(Q):
            field = g1[q, own, :].astype(F32)
            g4[q, own, :] = (field + act[:, QW * q : QW * q + QW]).astype(BF16)

    to_partner, to_across, relay = fine_copies(1, g4, lambda q: g4.at[q, mine, :])
    group = iota((1, QW), 1) // (QW // 4)
    pooled = dot(g4[:, mine, :].reshape(Q * CB, QW), pool[...])
    coarse = pooled[:CB]
    for q in range(1, Q):
        coarse = jnp.where(group == q, pooled[CB * q : CB * q + CB], coarse)
    coarse = (coarse * 0.25).astype(BF16)
    middle = coarse
    for layer, g in ((1, g2), (2, g3)):
        g[mine, :] = middle
        for copy in coarse_copies(layer - 1, g):
            copy.start()
        pack_rims(layer, dot(middle, sel2[...]))
        for copy in rim_copies(layer):
            copy.start()
        if layer == 1:
            for copy in to_across[: Q // 2] + to_partner:
                copy.start()
        w_copies[layer].wait()
        coarse_wait(g, coarse_recv.at[layer - 1])
        taps[:, :QW] = dot(w_v[layer].reshape(9 * CB, C), g[...])
        wait_bytes(rb.at[layer], rim_recv.at[layer])
        if layer == 1:
            for copy in to_across[Q // 2 :]:
                copy.start()
        half = range(Q // 2 * (layer - 1), Q // 2 * layer)
        for q in half:
            to_across[q].wait_recv()
            relay[q].start()
        rims = rim_sums(layer, S2, exp2)
        parts = []
        for rows in range(0, CB, 16):
            act = gelu(conv_rows(layer, S2, rows, rims))
            parts.append((middle[rows : rows + 16, :].astype(F32) + act).astype(BF16))
        middle = jnp.concatenate(parts, axis=0)

    g5[mine, :] = middle
    for copy in coarse_copies(2, g5):
        copy.start()
    picked = None
    for q in range(Q):
        own = (dot(middle, up[q]) + g4[q, mine, :].astype(F32)).astype(BF16)
        part = dot(own, sel1[QW * q : QW * q + QW, :])
        picked = part if picked is None else picked + part
    pack_rims(3, picked)
    for copy in rim_copies(3):
        copy.start()
    w_copies[3].wait()
    wait_bytes(g4.at[:, mine, :], partner_recv.at[1])
    for q in range(Q):
        relay[q].wait_recv()
    for index in range(2):
        for kind in range(3):
            wait_bytes(g4.at[:, mine, :], fine_send.at[index, kind])
    for layer in range(3):
        wait_bytes(rb.at[layer], rim_send.at[layer])
    for index in range(2):
        coarse_wait(g2, coarse_send.at[index])
    coarse_wait(g5, coarse_recv.at[2])
    for q in range(Q):
        joined[q] = (dot(g5[...], up[q]) + g4[q].astype(F32)).astype(BF16)
        taps[:, QW * q : QW * q + QW] = dot(w_v[3].reshape(9 * CB, C), joined[q])
    wait_bytes(rb.at[3], rim_recv.at[3])
    wait_bytes(rb.at[3], rim_send.at[3])
    coarse_wait(g5, coarse_send.at[2])
    rims = rim_sums(3, S1, exp1)
    for rows in range(0, CB, 16):
        act = gelu(conv_rows(3, S1, rows, rims))
        own = pl.ds(pl.multiple_of(chan * CB + rows, 16), 16)
        for q in range(Q):
            field = joined[q, own, :].astype(F32)
            out_ref[rows : rows + 16, QW * q : QW * q + QW] = (
                field + act[:, QW * q : QW * q + QW]
            ).astype(BF16)


def on_device(
    tiles,
    field_in,
    edge_codes,
    weight_enc,
    bias_enc,
    weight_mid_a,
    bias_mid_a,
    weight_mid_b,
    bias_mid_b,
    weight_dec,
    bias_dec,
):
    hbm = pl.BlockSpec(memory_space=pltpu.MemorySpace.HBM)
    vmem = pl.BlockSpec(memory_space=pltpu.MemorySpace.VMEM)
    dma = pltpu.SemaphoreType.DMA
    biases = [b.reshape(1, CB) for b in (bias_enc, bias_mid_a, bias_mid_b, bias_dec)]
    return pl.pallas_call(
        functools.partial(kernel, tiles),
        out_shape=jax.ShapeDtypeStruct((CB, S1 * S1), BF16),
        in_specs=[hbm] * 10,
        out_specs=vmem,
        scratch_shapes=[
            pltpu.SMEM((4, tiles), jnp.int32),
            pltpu.VMEM((Q, C, QW), BF16),
            pltpu.VMEM((C, QW), BF16),
            pltpu.VMEM((C, QW), BF16),
            pltpu.VMEM((Q, C, QW), BF16),
            pltpu.VMEM((C, QW), BF16),
            pltpu.VMEM((Q, C, QW), BF16),
            pltpu.VMEM((4, 9, CB, C), BF16),
            pltpu.VMEM((4, 1, CB), F32),
            pltpu.VMEM((4, CB, 128), F32),
            pltpu.VMEM((S1 * S1, 128), BF16),
            pltpu.VMEM((S2 * S2, 128), BF16),
            pltpu.VMEM((128, S1 * S1), BF16),
            pltpu.VMEM((128, S2 * S2), BF16),
            pltpu.VMEM((QW, QW), BF16),
            pltpu.VMEM((Q, QW, QW), BF16),
            pltpu.VMEM((4, 4, 16, 128), BF16),
            pltpu.VMEM((4, PEERS, 4, 16, 128), BF16),
            pltpu.VMEM((9 * CB, S1 * S1), F32),
            dma,
            dma,
            dma((4,)),
            dma((4,)),
            dma((2, 3)),
            dma((2,)),
            dma((2, 2, Q)),
            dma((3,)),
            dma((3,)),
            dma((4,)),
            dma((4,)),
        ],
        compiler_params=pltpu.CompilerParams(
            collective_id=0, has_side_effects=True, vmem_limit_bytes=62 * 1024 * 1024
        ),
        name="unet_window",
    )(
        edge_codes.T,
        field_in,
        weight_enc,
        weight_mid_a,
        weight_mid_b,
        weight_dec,
        *biases,
    )


def solution(mesh):
    weights = P(None, "chan", None)
    in_specs = (
        P("chan", "face"),
        P(),
        weights,
        P("chan"),
        weights,
        P("chan"),
        weights,
        P("chan"),
        weights,
        P("chan"),
    )
    return jax.shard_map(
        functools.partial(on_device, mesh.shape["face"]),
        mesh=mesh,
        in_specs=in_specs,
        out_specs=P("chan", "face"),
        check_vma=False,
    )
```

```python
import functools

import jax
import jax.numpy as jnp
from jax import lax
from jax.experimental import pallas as pl
from jax.experimental.pallas import tpu as pltpu
from jax.sharding import PartitionSpec as P

TILE_COLS = 4
CB = 64
PEERS = 4
C = CB * PEERS
S1 = 32
S2 = 16
Q = 4
QW = S1 * S1 // Q
GELU_A = 0.7978845608028654
GELU_B = 0.044715
MESH = pl.DeviceIdType.MESH
F32 = jnp.float32
BF16 = jnp.bfloat16


def iota(shape, dim):
    return lax.broadcasted_iota(jnp.int32, shape, dim)


def gelu(v):
    return 0.5 * v * (1.0 + jnp.tanh(GELU_A * (v + GELU_B * (v * v * v))))


def dot(a, b):
    return lax.dot_general(a, b, (((1,), (0,)), ((), ())), preferred_element_type=F32)


def one_hot(cond):
    return jnp.where(cond, 1.0, 0.0).astype(BF16)


def edge_position(edge, along, side):
    return jnp.where(
        edge == 0,
        along,
        jnp.where(
            edge == 1,
            (side - 1) * side + along,
            jnp.where(edge == 2, along * side, along * side + side - 1),
        ),
    )


def kernel(
    tiles,
    codes_hbm,
    x_hbm,
    w0_hbm,
    w1_hbm,
    w2_hbm,
    w3_hbm,
    b0_hbm,
    b1_hbm,
    b2_hbm,
    b3_hbm,
    out_ref,
    codes,
    g1,
    g2,
    g3,
    g4,
    g5,
    joined,
    w_v,
    b_v,
    bias_v,
    sel1,
    sel2,
    exp1,
    exp2,
    pool,
    up,
    sb,
    rb,
    taps,
    pre,
    codes_sem,
    x_sem,
    w_sem,
    b_sem,
    fine_send,
    partner_recv,
    fine_recv,
    coarse_send,
    coarse_recv,
    rim_send,
    rim_recv,
):
    tile = lax.axis_index("face")
    chan = lax.axis_index("chan")
    partner = chan + 1 - 2 * (chan % 2)
    across = (chan + 2) % 4
    diagonal = (partner + 2) % 4
    near = [
        (tile + TILE_COLS) % tiles,
        (tile + tiles - TILE_COLS) % tiles,
        (tile + 1) % tiles,
        (tile + tiles - 1) % tiles,
    ]
    mine = pl.ds(pl.multiple_of(chan * CB, CB), CB)
    across_rows = pl.ds(pl.multiple_of(across * CB, CB), CB)

    barrier = pltpu.get_barrier_semaphore()
    for peer in (partner, across, diagonal):
        pl.semaphore_signal(barrier, inc=1, device_id=(tile, peer), device_id_type=MESH)
    for side in range(4):
        for step in range(PEERS):
            peer = (chan + step) % PEERS
            pl.semaphore_signal(
                barrier, inc=1, device_id=(near[side], peer), device_id_type=MESH
            )

    codes_copy = pltpu.make_async_copy(codes_hbm, codes, codes_sem)
    codes_copy.start()
    x_copies = [
        pltpu.make_async_copy(x_hbm.at[:, pl.ds(q * QW, QW)], g1.at[q, mine, :], x_sem)
        for q in range(Q)
    ]
    for copy in x_copies:
        copy.start()
    w_copies = []
    b_copies = []
    for i, w in enumerate((w0_hbm, w1_hbm, w2_hbm, w3_hbm)):
        w_copies.append(pltpu.make_async_copy(w, w_v.at[i], w_sem.at[i]))
    for i, b in enumerate((b0_hbm, b1_hbm, b2_hbm, b3_hbm)):
        b_copies.append(pltpu.make_async_copy(b, b_v.at[i], b_sem.at[i]))

    lane = iota((1, 128), 1)
    slot = lane // 32
    along = lane % 32

    def wait_bytes(ref, sem):
        pltpu.make_async_copy(ref, ref, sem).wait()

    def pick_table(code, size, sel):
        place = jnp.where(code >= 4, size - 1 - along, along)
        cell = jnp.where(along < size, edge_position(code % 4, place, size), -1)
        sel[...] = one_hot(iota((size * size, 128), 0) == cell)

    def other_tables():
        row = iota((128, 1), 0)
        for size, exp in ((S1, exp1), (S2, exp2)):
            cell = jnp.where(
                row % 32 < size, edge_position(row // 32, row % 32, size), -1
            )
            exp[...] = one_hot(iota((128, size * size), 1) == cell)
        cell = iota((QW, QW), 0)
        pool[...] = one_hot(
            (cell // S1 // 2) * S2 + (cell % S1) // 2 == iota((QW, QW), 1) % (QW // 4)
        )
        cell = iota((1, QW), 1)
        cell = (cell // S1 // 2) * S2 + (cell % S1) // 2
        for q in range(Q):
            up[q] = one_hot(iota((QW, QW), 0) == cell + q * (QW // 4))
        eye = iota((CB, CB), 0) == iota((CB, CB), 1)
        for copy in b_copies:
            copy.wait()
        for i in range(4):
            column = jnp.sum(
                jnp.where(eye, jnp.broadcast_to(b_v[i], (CB, CB)), 0.0), axis=1, keepdims=True
            )
            bias_v[i] = jnp.broadcast_to(column, (CB, 128))

    def pack_rims(layer, picked):
        for side in range(4):
            block = None
            for group in range(4):
                part = picked[16 * group : 16 * group + 16, :]
                shift = (32 * (group - side)) % 128
                if shift:
                    part = pltpu.roll(part, shift, 1)
                block = part if block is None else jnp.where(slot == group, part, block)
            sb[layer, side] = block.astype(BF16)

    def rim_copies(layer):
        copies = []
        for step in range(PEERS):
            for side in range(4):
                peer = (chan + step) % PEERS
                copies.append(
                    pltpu.make_async_remote_copy(
                        src_ref=sb.at[layer, side],
                        dst_ref=rb.at[layer, chan, side],
                        send_sem=rim_send.at[layer],
                        recv_sem=rim_recv.at[layer],
                        device_id=(near[side], peer),
                        device_id_type=MESH,
                    )
                )
        return copies

    def fine_copies(index, g, source):
        def copies_to(kind, peer, rows, source, recv):
            return [
                pltpu.make_async_remote_copy(
                    src_ref=source(q),
                    dst_ref=g.at[q, rows, :],
                    send_sem=fine_send.at[index, kind],
                    recv_sem=recv[q],
                    device_id=(tile, peer),
                    device_id_type=MESH,
                )
                for q in range(Q)
            ]

        return (
            copies_to(0, partner, mine, source, [partner_recv.at[index]] * Q),
            copies_to(1, across, mine, source, [fine_recv.at[index, 0, q] for q in range(Q)]),
            copies_to(
                2,
                partner,
                across_rows,
                lambda q: g.at[q, across_rows, :],
                [fine_recv.at[index, 1, q] for q in range(Q)],
            ),
        )

    def coarse_copies(index, g):
        return [
            pltpu.make_async_remote_copy(
                src_ref=g.at[mine, :],
                dst_ref=g.at[mine, :],
                send_sem=coarse_send.at[index],
                recv_sem=coarse_recv.at[index],
                device_id=(tile, peer),
                device_id_type=MESH,
            )
            for peer in (across, diagonal, partner)
        ]

    def coarse_wait(g, sem):
        wait_bytes(g.at[pl.ds(0, 3 * CB), :], sem)

    def rim_sums(layer, size, exp):
        blocks = []
        for source in range(PEERS):
            parts = [rb[layer, source, side].astype(F32) for side in range(4)]
            for group in range(4):
                block = None
                for side in range(4):
                    part = parts[side]
                    shift = (32 * (side - group)) % 128
                    if shift:
                        part = pltpu.roll(part, shift, 1)
                    block = part if block is None else jnp.where(slot == side, part, block)
                blocks.append(block.astype(BF16))
        rims = jnp.concatenate(blocks, axis=0)
        r = dot(w_v[layer].reshape(9 * CB, C), rims)
        r = [r[CB * t : CB * t + CB, :] for t in range(9)]

        def by_side(north, south, west, east):
            return jnp.where(
                slot == 0,
                r[north],
                jnp.where(slot == 1, r[south], jnp.where(slot == 2, r[west], r[east])),
            )

        before = jnp.where(along == 0, 0.0, pltpu.roll(by_side(0, 6, 0, 2), 1, 1))
        after = jnp.where(along == size - 1, 0.0, pltpu.roll(by_side(2, 8, 6, 8), 127, 1))
        total = before + by_side(1, 7, 3, 5) + after
        high = total.astype(BF16)
        low = (total - high.astype(F32)).astype(BF16)
        spread = dot(jnp.concatenate([high, low], axis=0), exp[...])
        return spread[:CB] + spread[CB:]

    def conv_rows(layer, size, rows):
        cells = size * size
        place = iota((1, cells), 1)
        column = place % size
        sums = []
        for dx in range(3):
            t = [taps[pl.ds(CB * (3 * dy + dx) + rows, 16), :cells] for dy in range(3)]
            above = jnp.where(place >= size, pltpu.roll(t[0], size, 1), 0.0)
            below = jnp.where(place < cells - size, pltpu.roll(t[2], cells - size, 1), 0.0)
            sums.append(t[1] + (above + below))
        left = jnp.where(column == 0, 0.0, pltpu.roll(sums[0], 1, 1))
        right = jnp.where(column == size - 1, 0.0, pltpu.roll(sums[2], cells - 1, 1))
        bias = bias_v[layer, rows : rows + 16, 0:1]
        pre[rows : rows + 16, :cells] = (sums[1] + (left + right)) + bias

    def inner_sums(layer, size):
        for rows in range(0, CB, 16):
            conv_rows(layer, size, rows)

    def activation(size, rows, rims):
        return gelu(pre[rows : rows + 16, : size * size] + rims[rows : rows + 16, :])

    to_partner, to_across, relay = fine_copies(0, g1, lambda q: x_hbm.at[:, pl.ds(q * QW, QW)])
    for copy in b_copies + w_copies:
        copy.start()
    codes_copy.wait()
    codes_here = [codes[side, near[side]] for side in range(4)]
    code = jnp.where(
        slot == 0,
        codes_here[0],
        jnp.where(slot == 1, codes_here[1], jnp.where(slot == 2, codes_here[2], codes_here[3])),
    )
    pick_table(code, S1, sel1)
    wait_bytes(g1.at[:, mine, :], x_sem)
    picked = sum(dot(g1[q, mine, :], sel1[QW * q : QW * q + QW, :]) for q in range(Q))
    pack_rims(0, picked)
    pl.semaphore_wait(barrier, 3 + 4 * PEERS)
    for copy in rim_copies(0):
        copy.start()
    for copy in to_across + to_partner:
        copy.start()
    pick_table(code, S2, sel2)
    other_tables()
    w_copies[0].wait()
    for q in range(Q):
        to_across[q].wait_recv()
        relay[q].start()
    wait_bytes(g1.at[:, mine, :], partner_recv.at[0])
    for q in range(Q):
        relay[q].wait_recv()
        taps[:, QW * q : QW * q + QW] = dot(w_v[0].reshape(9 * CB, C), g1[q])
    inner_sums(0, S1)
    wait_bytes(rb.at[0], rim_recv.at[0])
    rims = rim_sums(0, S1, exp1)
    for rows in range(0, CB, 16):
        act = activation(S1, rows, rims)
        own = pl.ds(pl.multiple_of(chan * CB + rows, 16), 16)
        for q in range(Q):
            field = g1[q, own, :].astype(F32)
            g4[q, own, :] = (field + act[:, QW * q : QW * q + QW]).astype(BF16)

    to_partner, to_across, relay = fine_copies(1, g4, lambda q: g4.at[q, mine, :])
    group = iota((1, QW), 1) // (QW // 4)
    pooled = dot(g4[:, mine, :].reshape(Q * CB, QW), pool[...])
    coarse = pooled[:CB]
    for q in range(1, Q):
        coarse = jnp.where(group == q, pooled[CB * q : CB * q + CB], coarse)
    coarse = (coarse * 0.25).astype(BF16)
    middle = coarse
    for layer, g in ((1, g2), (2, g3)):
        g[mine, :] = middle
        pack_rims(layer, dot(middle, sel2[...]))
        for copy in rim_copies(layer):
            copy.start()
        for copy in coarse_copies(layer - 1, g):
            copy.start()
        if layer == 1:
            for copy in to_across + to_partner:
                copy.start()
        else:
            for q in range(Q):
                to_across[q].wait_recv()
                relay[q].start()
        w_copies[layer].wait()
        coarse_wait(g, coarse_recv.at[layer - 1])
        taps[:, :QW] = dot(w_v[layer].reshape(9 * CB, C), g[...])
        inner_sums(layer, S2)
        wait_bytes(rb.at[layer], rim_recv.at[layer])
        rims = rim_sums(layer, S2, exp2)
        parts = []
        for rows in range(0, CB, 16):
            act = activation(S2, rows, rims)
            parts.append((middle[rows : rows + 16, :].astype(F32) + act).astype(BF16))
        middle = jnp.concatenate(parts, axis=0)

    g5[mine, :] = middle
    picked = None
    for q in range(Q):
        own = (dot(middle, up[q]) + g4[q, mine, :].astype(F32)).astype(BF16)
        part = dot(own, sel1[QW * q : QW * q + QW, :])
        picked = part if picked is None else picked + part
    pack_rims(3, picked)
    for copy in rim_copies(3):
        copy.start()
    for copy in coarse_copies(2, g5):
        copy.start()
    w_copies[3].wait()
    wait_bytes(g4.at[:, mine, :], partner_recv.at[1])
    for q in range(Q):
        relay[q].wait_recv()
    for index in range(2):
        for kind in range(3):
            wait_bytes(g4.at[:, mine, :], fine_send.at[index, kind])
    for layer in range(3):
        wait_bytes(rb.at[layer], rim_send.at[layer])
    for index in range(2):
        coarse_wait(g2, coarse_send.at[index])
    coarse_wait(g5, coarse_recv.at[2])
    for q in range(Q):
        joined[q] = (dot(g5[...], up[q]) + g4[q].astype(F32)).astype(BF16)
        taps[:, QW * q : QW * q + QW] = dot(w_v[3].reshape(9 * CB, C), joined[q])
    inner_sums(3, S1)
    wait_bytes(rb.at[3], rim_send.at[3])
    coarse_wait(g5, coarse_send.at[2])
    wait_bytes(rb.at[3], rim_recv.at[3])
    rims = rim_sums(3, S1, exp1)
    for rows in range(0, CB, 16):
        act = activation(S1, rows, rims)
        own = pl.ds(pl.multiple_of(chan * CB + rows, 16), 16)
        for q in range(Q):
            field = joined[q, own, :].astype(F32)
            out_ref[rows : rows + 16, QW * q : QW * q + QW] = (
                field + act[:, QW * q : QW * q + QW]
            ).astype(BF16)


def on_device(
    tiles,
    field_in,
    edge_codes,
    weight_enc,
    bias_enc,
    weight_mid_a,
    bias_mid_a,
    weight_mid_b,
    bias_mid_b,
    weight_dec,
    bias_dec,
):
    hbm = pl.BlockSpec(memory_space=pltpu.MemorySpace.HBM)
    vmem = pl.BlockSpec(memory_space=pltpu.MemorySpace.VMEM)
    dma = pltpu.SemaphoreType.DMA
    biases = [b.reshape(1, CB) for b in (bias_enc, bias_mid_a, bias_mid_b, bias_dec)]
    return pl.pallas_call(
        functools.partial(kernel, tiles),
        out_shape=pltpu.MemorySpace.VMEM((CB, S1 * S1), BF16),
        in_specs=[hbm] * 10,
        out_specs=vmem,
        scratch_shapes=[
            pltpu.SMEM((4, tiles), jnp.int32),
            pltpu.VMEM((Q, C, QW), BF16),
            pltpu.VMEM((C, QW), BF16),
            pltpu.VMEM((C, QW), BF16),
            pltpu.VMEM((Q, C, QW), BF16),
            pltpu.VMEM((C, QW), BF16),
            pltpu.VMEM((Q, C, QW), BF16),
            pltpu.VMEM((4, 9, CB, C), BF16),
            pltpu.VMEM((4, 1, CB), F32),
            pltpu.VMEM((4, CB, 128), F32),
            pltpu.VMEM((S1 * S1, 128), BF16),
            pltpu.VMEM((S2 * S2, 128), BF16),
            pltpu.VMEM((128, S1 * S1), BF16),
            pltpu.VMEM((128, S2 * S2), BF16),
            pltpu.VMEM((QW, QW), BF16),
            pltpu.VMEM((Q, QW, QW), BF16),
            pltpu.VMEM((4, 4, 16, 128), BF16),
            pltpu.VMEM((4, PEERS, 4, 16, 128), BF16),
            pltpu.VMEM((9 * CB, S1 * S1), F32),
            pltpu.VMEM((CB, S1 * S1), F32),
            dma,
            dma,
            dma((4,)),
            dma((4,)),
            dma((2, 3)),
            dma((2,)),
            dma((2, 2, Q)),
            dma((3,)),
            dma((3,)),
            dma((4,)),
            dma((4,)),
        ],
        compiler_params=pltpu.CompilerParams(
            collective_id=0, has_side_effects=True, vmem_limit_bytes=62 * 1024 * 1024
        ),
        name="unet_window",
    )(
        edge_codes.T,
        field_in,
        weight_enc,
        weight_mid_a,
        weight_mid_b,
        weight_dec,
        *biases,
    )


def solution(mesh):
    weights = P(None, "chan", None)
    in_specs = (
        P("chan", "face"),
        P(),
        weights,
        P("chan"),
        weights,
        P("chan"),
        weights,
        P("chan"),
        weights,
        P("chan"),
    )
    return jax.shard_map(
        functools.partial(on_device, mesh.shape["face"]),
        mesh=mesh,
        in_specs=in_specs,
        out_specs=P("chan", "face"),
        check_vma=False,
    )
```

```python
import functools

import jax
import jax.numpy as jnp
from jax import lax
from jax.experimental import pallas as pl
from jax.experimental.pallas import tpu as pltpu
from jax.sharding import PartitionSpec as P

TILE_COLS = 4
CB = 64
PEERS = 4
C = CB * PEERS
S1 = 32
S2 = 16
Q = 4
QW = S1 * S1 // Q
GELU_A = 0.7978845608028654
GELU_B = 0.044715
MESH = pl.DeviceIdType.MESH
F32 = jnp.float32
BF16 = jnp.bfloat16


def iota(shape, dim):
    return lax.broadcasted_iota(jnp.int32, shape, dim)


def gelu(v):
    return 0.5 * v * (1.0 + jnp.tanh(GELU_A * (v + GELU_B * (v * v * v))))


def dot(a, b):
    return lax.dot_general(a, b, (((1,), (0,)), ((), ())), preferred_element_type=F32)


def one_hot(cond):
    return jnp.where(cond, 1.0, 0.0).astype(BF16)


def edge_position(edge, along, side):
    return jnp.where(
        edge == 0,
        along,
        jnp.where(
            edge == 1,
            (side - 1) * side + along,
            jnp.where(edge == 2, along * side, along * side + side - 1),
        ),
    )


def kernel(
    tiles,
    codes_hbm,
    x_hbm,
    w0_hbm,
    w1_hbm,
    w2_hbm,
    w3_hbm,
    b0_hbm,
    b1_hbm,
    b2_hbm,
    b3_hbm,
    out_ref,
    codes,
    g1,
    g2,
    g3,
    g4,
    g5,
    joined,
    w_v,
    b_v,
    bias_v,
    sel1,
    sel_enc,
    sel_a,
    sel_b,
    nxt_enc,
    nxt_a,
    nxt_b,
    exp1,
    exp2,
    pool,
    up,
    sb,
    rb,
    taps,
    pre,
    codes_sem,
    x_sem,
    w_sem,
    b_sem,
    fine_send,
    partner_recv,
    fine_recv,
    coarse_send,
    coarse_recv,
    rim_send,
    rim_recv,
):
    tile = lax.axis_index("face")
    chan = lax.axis_index("chan")
    partner = chan + 1 - 2 * (chan % 2)
    across = (chan + 2) % 4
    diagonal = (partner + 2) % 4
    near = [
        (tile + TILE_COLS) % tiles,
        (tile + tiles - TILE_COLS) % tiles,
        (tile + 1) % tiles,
        (tile + tiles - 1) % tiles,
    ]
    mine = pl.ds(pl.multiple_of(chan * CB, CB), CB)
    across_rows = pl.ds(pl.multiple_of(across * CB, CB), CB)

    barrier = pltpu.get_barrier_semaphore()
    for peer in (partner, across, diagonal):
        pl.semaphore_signal(barrier, inc=1, device_id=(tile, peer), device_id_type=MESH)
    for side in range(4):
        for step in range(PEERS):
            peer = (chan + step) % PEERS
            pl.semaphore_signal(
                barrier, inc=1, device_id=(near[side], peer), device_id_type=MESH
            )

    codes_copy = pltpu.make_async_copy(codes_hbm, codes, codes_sem)
    codes_copy.start()
    x_copies = [
        pltpu.make_async_copy(x_hbm.at[:, pl.ds(q * QW, QW)], g1.at[q, mine, :], x_sem)
        for q in range(Q)
    ]
    for copy in x_copies:
        copy.start()
    w_copies = []
    b_copies = []
    for i, w in enumerate((w0_hbm, w1_hbm, w2_hbm, w3_hbm)):
        w_copies.append(pltpu.make_async_copy(w, w_v.at[i], w_sem.at[i]))
    for i, b in enumerate((b0_hbm, b1_hbm, b2_hbm, b3_hbm)):
        b_copies.append(pltpu.make_async_copy(b, b_v.at[i], b_sem.at[i]))

    lane = iota((1, 128), 1)
    slot = lane // 32
    along = lane % 32

    def wait_bytes(ref, sem):
        pltpu.make_async_copy(ref, ref, sem).wait()

    def pick_tables(code):
        edge = code % 4
        place = jnp.where(code >= 4, S2 - 1 - along, along)
        cell = edge_position(edge, place, S2)
        sel_a[...] = one_hot(iota((S2 * S2, 128), 0) == jnp.where(along < S2, cell, -1))
        corner = 2 * (cell // S2) * S1 + 2 * (cell % S2)
        for part in range(4):
            fine = jnp.where(along < S2, corner + part // 2 * S1 + part % 2, -1)
            sel_enc[:, 128 * part : 128 * part + 128] = one_hot(iota((S1 * S1, 128), 0) == fine)
        place = jnp.where(code >= 4, S1 - 1 - along, along)
        sel_b[...] = one_hot(iota((S2 * S2, 128), 0) == edge_position(edge, place // 2, S2))

    def other_tables():
        row = iota((128, 1), 0)
        for size, exp in ((S1, exp1), (S2, exp2)):
            cell = jnp.where(
                row % 32 < size, edge_position(row // 32, row % 32, size), -1
            )
            exp[...] = one_hot(iota((128, size * size), 1) == cell)
        nxt_enc[...] = dot(exp1[...], sel_enc[...]).astype(BF16)
        nxt_a[...] = dot(exp2[...], sel_a[...]).astype(BF16)
        nxt_b[...] = dot(exp2[...], sel_b[...]).astype(BF16)
        cell = iota((QW, QW), 0)
        pool[...] = one_hot(
            (cell // S1 // 2) * S2 + (cell % S1) // 2 == iota((QW, QW), 1) % (QW // 4)
        )
        cell = iota((1, QW), 1)
        cell = (cell // S1 // 2) * S2 + (cell % S1) // 2
        for q in range(Q):
            up[q] = one_hot(iota((QW, QW), 0) == cell + q * (QW // 4))
        eye = iota((CB, CB), 0) == iota((CB, CB), 1)
        for copy in b_copies:
            copy.wait()
        for i in range(4):
            column = jnp.sum(
                jnp.where(eye, jnp.broadcast_to(b_v[i], (CB, CB)), 0.0), axis=1, keepdims=True
            )
            bias_v[i] = jnp.broadcast_to(column, (CB, 128))

    def pack_rims(layer, picked):
        for side in range(4):
            block = None
            for group in range(4):
                part = picked[16 * group : 16 * group + 16, :]
                shift = (32 * (group - side)) % 128
                if shift:
                    part = pltpu.roll(part, shift, 1)
                block = part if block is None else jnp.where(slot == group, part, block)
            sb[layer, side] = block.astype(BF16)

    def rim_copies(layer):
        copies = []
        for peer in (across, diagonal, partner, chan):
            for side in range(4):
                copies.append(
                    pltpu.make_async_remote_copy(
                        src_ref=sb.at[layer, side],
                        dst_ref=rb.at[layer, chan, side],
                        send_sem=rim_send.at[layer],
                        recv_sem=rim_recv.at[layer],
                        device_id=(near[side], peer),
                        device_id_type=MESH,
                    )
                )
        return copies

    def fine_copies(index, g, source):
        def copies_to(kind, peer, rows, source, recv):
            return [
                pltpu.make_async_remote_copy(
                    src_ref=source(q),
                    dst_ref=g.at[q, rows, :],
                    send_sem=fine_send.at[index, kind],
                    recv_sem=recv[q],
                    device_id=(tile, peer),
                    device_id_type=MESH,
                )
                for q in range(Q)
            ]

        return (
            copies_to(0, partner, mine, source, [partner_recv.at[index]] * Q),
            copies_to(1, across, mine, source, [fine_recv.at[index, 0, q] for q in range(Q)]),
            copies_to(
                2,
                partner,
                across_rows,
                lambda q: g.at[q, across_rows, :],
                [fine_recv.at[index, 1, q] for q in range(Q)],
            ),
        )

    def coarse_copies(index, g):
        return [
            pltpu.make_async_remote_copy(
                src_ref=g.at[mine, :],
                dst_ref=g.at[mine, :],
                send_sem=coarse_send.at[index],
                recv_sem=coarse_recv.at[index],
                device_id=(tile, peer),
                device_id_type=MESH,
            )
            for peer in (across, diagonal, partner)
        ]

    def coarse_wait(g, sem):
        wait_bytes(g.at[pl.ds(0, 3 * CB), :], sem)

    def in_two(v):
        high = v.astype(BF16)
        return jnp.concatenate([high, (v - high.astype(F32)).astype(BF16)], axis=0)

    def take(two, table):
        both = dot(two, table)
        return both[:CB] + both[CB:]

    def rim_sums(layer, size):
        blocks = []
        for source in range(PEERS):
            parts = [rb[layer, source, side].astype(F32) for side in range(4)]
            for group in range(4):
                block = None
                for side in range(4):
                    part = parts[side]
                    shift = (32 * (side - group)) % 128
                    if shift:
                        part = pltpu.roll(part, shift, 1)
                    block = part if block is None else jnp.where(slot == side, part, block)
                blocks.append(block.astype(BF16))
        rims = jnp.concatenate(blocks, axis=0)
        r = dot(w_v[layer].reshape(9 * CB, C), rims)
        r = [r[CB * t : CB * t + CB, :] for t in range(9)]

        def by_side(north, south, west, east):
            return jnp.where(
                slot == 0,
                r[north],
                jnp.where(slot == 1, r[south], jnp.where(slot == 2, r[west], r[east])),
            )

        before = jnp.where(along == 0, 0.0, pltpu.roll(by_side(0, 6, 0, 2), 1, 1))
        after = jnp.where(along == size - 1, 0.0, pltpu.roll(by_side(2, 8, 6, 8), 127, 1))
        total = before + by_side(1, 7, 3, 5) + after
        return in_two(total)

    def conv_rows(layer, size, rows):
        cells = size * size
        place = iota((1, cells), 1)
        column = place % size
        sums = []
        for dx in range(3):
            t = [taps[pl.ds(CB * (3 * dy + dx) + rows, 16), :cells] for dy in range(3)]
            above = jnp.where(place >= size, pltpu.roll(t[0], size, 1), 0.0)
            below = jnp.where(place < cells - size, pltpu.roll(t[2], cells - size, 1), 0.0)
            sums.append(t[1] + (above + below))
        left = jnp.where(column == 0, 0.0, pltpu.roll(sums[0], 1, 1))
        right = jnp.where(column == size - 1, 0.0, pltpu.roll(sums[2], cells - 1, 1))
        bias = bias_v[layer, rows : rows + 16, 0:1]
        pre[rows : rows + 16, :cells] = (sums[1] + (left + right)) + bias

    def inner_sums(layer, size):
        for rows in range(0, CB, 16):
            conv_rows(layer, size, rows)

    def activation(size, rows, rims):
        return gelu(pre[rows : rows + 16, : size * size] + rims[rows : rows + 16, :])

    to_partner, to_across, relay = fine_copies(0, g1, lambda q: x_hbm.at[:, pl.ds(q * QW, QW)])
    for copy in b_copies + w_copies:
        copy.start()
    codes_copy.wait()
    codes_here = [codes[side, near[side]] for side in range(4)]
    code = jnp.where(
        slot == 0,
        codes_here[0],
        jnp.where(slot == 1, codes_here[1], jnp.where(slot == 2, codes_here[2], codes_here[3])),
    )
    place = jnp.where(code >= 4, S1 - 1 - along, along)
    cell = edge_position(code % 4, place, S1)
    sel1[...] = one_hot(iota((S1 * S1, 128), 0) == cell)
    wait_bytes(g1.at[:, mine, :], x_sem)
    picked = sum(dot(g1[q, mine, :], sel1[QW * q : QW * q + QW, :]) for q in range(Q))
    pack_rims(0, picked)
    pl.semaphore_wait(barrier, 3 + 4 * PEERS)
    for copy in rim_copies(0):
        copy.start()
    for copy in to_across + to_partner:
        copy.start()
    pick_tables(code)
    other_tables()
    w_copies[0].wait()
    for q in range(Q):
        to_across[q].wait_recv()
        relay[q].start()
    wait_bytes(g1.at[:, mine, :], partner_recv.at[0])
    for q in range(Q):
        relay[q].wait_recv()
        taps[:, QW * q : QW * q + QW] = dot(w_v[0].reshape(9 * CB, C), g1[q])
    inner_sums(0, S1)
    sums = take(in_two(pre[...]), sel_enc[...])
    field = sum(dot(g1[q, mine, :], sel_enc[QW * q : QW * q + QW, :]) for q in range(Q))
    wait_bytes(rb.at[0], rim_recv.at[0])
    two = rim_sums(0, S1)
    edge = (field + gelu(sums + take(two, nxt_enc[...]))).astype(BF16).astype(F32)
    edge = (edge[:, :128] + edge[:, 128:256]) + (edge[:, 256:384] + edge[:, 384:])
    pack_rims(1, edge * 0.25)
    for copy in rim_copies(1):
        copy.start()
    rims = take(two, exp1[...])
    for rows in range(0, CB, 16):
        act = activation(S1, rows, rims)
        own = pl.ds(pl.multiple_of(chan * CB + rows, 16), 16)
        for q in range(Q):
            field = g1[q, own, :].astype(F32)
            g4[q, own, :] = (field + act[:, QW * q : QW * q + QW]).astype(BF16)

    to_partner, to_across, relay = fine_copies(1, g4, lambda q: g4.at[q, mine, :])
    group = iota((1, QW), 1) // (QW // 4)
    pooled = dot(g4[:, mine, :].reshape(Q * CB, QW), pool[...])
    coarse = pooled[:CB]
    for q in range(1, Q):
        coarse = jnp.where(group == q, pooled[CB * q : CB * q + CB], coarse)
    coarse = (coarse * 0.25).astype(BF16)
    middle = coarse
    encoded = sum(dot(g4[q, mine, :], sel1[QW * q : QW * q + QW, :]) for q in range(Q))
    for layer, g in ((1, g2), (2, g3)):
        g[mine, :] = middle
        for copy in coarse_copies(layer - 1, g):
            copy.start()
        if layer == 1:
            for copy in to_across + to_partner:
                copy.start()
        else:
            for q in range(Q):
                to_across[q].wait_recv()
                relay[q].start()
        w_copies[layer].wait()
        coarse_wait(g, coarse_recv.at[layer - 1])
        taps[:, :QW] = dot(w_v[layer].reshape(9 * CB, C), g[...])
        inner_sums(layer, S2)
        sel, nxt = ((sel_a, nxt_a), (sel_b, nxt_b))[layer - 1]
        sums = take(in_two(pre[:, :QW]), sel[...])
        field = dot(middle, sel[...])
        wait_bytes(rb.at[layer], rim_recv.at[layer])
        two = rim_sums(layer, S2)
        edge = (field + gelu(sums + take(two, nxt[...]))).astype(BF16).astype(F32)
        if layer == 2:
            edge = edge + encoded
        pack_rims(layer + 1, edge)
        for copy in rim_copies(layer + 1):
            copy.start()
        rims = take(two, exp2[...])
        parts = []
        for rows in range(0, CB, 16):
            act = activation(S2, rows, rims)
            parts.append((middle[rows : rows + 16, :].astype(F32) + act).astype(BF16))
        middle = jnp.concatenate(parts, axis=0)

    g5[mine, :] = middle
    for copy in coarse_copies(2, g5):
        copy.start()
    w_copies[3].wait()
    wait_bytes(g4.at[:, mine, :], partner_recv.at[1])
    for q in range(Q):
        relay[q].wait_recv()
    for index in range(2):
        for kind in range(3):
            wait_bytes(g4.at[:, mine, :], fine_send.at[index, kind])
    for layer in range(3):
        wait_bytes(rb.at[layer], rim_send.at[layer])
    for index in range(2):
        coarse_wait(g2, coarse_send.at[index])
    coarse_wait(g5, coarse_recv.at[2])
    for q in range(Q):
        joined[q] = (dot(g5[...], up[q]) + g4[q].astype(F32)).astype(BF16)
        taps[:, QW * q : QW * q + QW] = dot(w_v[3].reshape(9 * CB, C), joined[q])
    inner_sums(3, S1)
    wait_bytes(rb.at[3], rim_send.at[3])
    coarse_wait(g5, coarse_send.at[2])
    wait_bytes(rb.at[3], rim_recv.at[3])
    rims = take(rim_sums(3, S1), exp1[...])
    for rows in range(0, CB, 16):
        act = activation(S1, rows, rims)
        own = pl.ds(pl.multiple_of(chan * CB + rows, 16), 16)
        for q in range(Q):
            field = joined[q, own, :].astype(F32)
            out_ref[rows : rows + 16, QW * q : QW * q + QW] = (
                field + act[:, QW * q : QW * q + QW]
            ).astype(BF16)


def on_device(
    tiles,
    field_in,
    edge_codes,
    weight_enc,
    bias_enc,
    weight_mid_a,
    bias_mid_a,
    weight_mid_b,
    bias_mid_b,
    weight_dec,
    bias_dec,
):
    hbm = pl.BlockSpec(memory_space=pltpu.MemorySpace.HBM)
    vmem = pl.BlockSpec(memory_space=pltpu.MemorySpace.VMEM)
    dma = pltpu.SemaphoreType.DMA
    biases = [b.reshape(1, CB) for b in (bias_enc, bias_mid_a, bias_mid_b, bias_dec)]
    return pl.pallas_call(
        functools.partial(kernel, tiles),
        out_shape=pltpu.MemorySpace.VMEM((CB, S1 * S1), BF16),
        in_specs=[hbm] * 10,
        out_specs=vmem,
        scratch_shapes=[
            pltpu.SMEM((4, tiles), jnp.int32),
            pltpu.VMEM((Q, C, QW), BF16),
            pltpu.VMEM((C, QW), BF16),
            pltpu.VMEM((C, QW), BF16),
            pltpu.VMEM((Q, C, QW), BF16),
            pltpu.VMEM((C, QW), BF16),
            pltpu.VMEM((Q, C, QW), BF16),
            pltpu.VMEM((4, 9, CB, C), BF16),
            pltpu.VMEM((4, 1, CB), F32),
            pltpu.VMEM((4, CB, 128), F32),
            pltpu.VMEM((S1 * S1, 128), BF16),
            pltpu.VMEM((S1 * S1, 4 * 128), BF16),
            pltpu.VMEM((S2 * S2, 128), BF16),
            pltpu.VMEM((S2 * S2, 128), BF16),
            pltpu.VMEM((128, 4 * 128), BF16),
            pltpu.VMEM((128, 128), BF16),
            pltpu.VMEM((128, 128), BF16),
            pltpu.VMEM((128, S1 * S1), BF16),
            pltpu.VMEM((128, S2 * S2), BF16),
            pltpu.VMEM((QW, QW), BF16),
            pltpu.VMEM((Q, QW, QW), BF16),
            pltpu.VMEM((4, 4, 16, 128), BF16),
            pltpu.VMEM((4, PEERS, 4, 16, 128), BF16),
            pltpu.VMEM((9 * CB, S1 * S1), F32),
            pltpu.VMEM((CB, S1 * S1), F32),
            dma,
            dma,
            dma((4,)),
            dma((4,)),
            dma((2, 3)),
            dma((2,)),
            dma((2, 2, Q)),
            dma((3,)),
            dma((3,)),
            dma((4,)),
            dma((4,)),
        ],
        compiler_params=pltpu.CompilerParams(
            collective_id=0, has_side_effects=True, vmem_limit_bytes=62 * 1024 * 1024
        ),
        name="unet_window",
    )(
        edge_codes.T,
        field_in,
        weight_enc,
        weight_mid_a,
        weight_mid_b,
        weight_dec,
        *biases,
    )


def solution(mesh):
    weights = P(None, "chan", None)
    in_specs = (
        P("chan", "face"),
        P(),
        weights,
        P("chan"),
        weights,
        P("chan"),
        weights,
        P("chan"),
        weights,
        P("chan"),
    )
    return jax.shard_map(
        functools.partial(on_device, mesh.shape["face"]),
        mesh=mesh,
        in_specs=in_specs,
        out_specs=P("chan", "face"),
        check_vma=False,
    )
```

```python
import functools

import jax
import jax.numpy as jnp
from jax import lax
from jax.experimental import pallas as pl
from jax.experimental.pallas import tpu as pltpu
from jax.sharding import PartitionSpec as P

TILE_COLS = 4
CB = 64
PEERS = 4
C = CB * PEERS
S1 = 32
S2 = 16
Q = 4
QW = S1 * S1 // Q
GELU_A = 0.7978845608028654
GELU_B = 0.044715
MESH = pl.DeviceIdType.MESH
F32 = jnp.float32
BF16 = jnp.bfloat16


def iota(shape, dim):
    return lax.broadcasted_iota(jnp.int32, shape, dim)


def gelu(v):
    return 0.5 * v * (1.0 + jnp.tanh(GELU_A * (v + GELU_B * (v * v * v))))


def dot(a, b):
    return lax.dot_general(a, b, (((1,), (0,)), ((), ())), preferred_element_type=F32)


def one_hot(cond):
    return jnp.where(cond, 1.0, 0.0).astype(BF16)


def edge_position(edge, along, side):
    return jnp.where(
        edge == 0,
        along,
        jnp.where(
            edge == 1,
            (side - 1) * side + along,
            jnp.where(edge == 2, along * side, along * side + side - 1),
        ),
    )


def kernel(
    tiles,
    codes_hbm,
    x_hbm,
    w0_hbm,
    w1_hbm,
    w2_hbm,
    w3_hbm,
    b0_hbm,
    b1_hbm,
    b2_hbm,
    b3_hbm,
    out_ref,
    codes,
    g1,
    g2,
    g3,
    g4,
    g5,
    joined,
    w_v,
    b_v,
    bias_v,
    sel1,
    sel_enc,
    sel_a,
    sel_b,
    nxt_enc,
    nxt_a,
    nxt_b,
    exp1,
    exp2,
    pool,
    up,
    sb,
    rb,
    taps,
    pre,
    codes_sem,
    x_sem,
    w_sem,
    b_sem,
    fine_send,
    partner_recv,
    fine_recv,
    coarse_send,
    across_recv,
    coarse_recv,
    rim_send,
    rim_recv,
):
    tile = lax.axis_index("face")
    chan = lax.axis_index("chan")
    partner = chan + 1 - 2 * (chan % 2)
    across = (chan + 2) % 4
    diagonal = (partner + 2) % 4
    near = [
        (tile + TILE_COLS) % tiles,
        (tile + tiles - TILE_COLS) % tiles,
        (tile + 1) % tiles,
        (tile + tiles - 1) % tiles,
    ]
    mine = pl.ds(pl.multiple_of(chan * CB, CB), CB)
    across_rows = pl.ds(pl.multiple_of(across * CB, CB), CB)

    barrier = pltpu.get_barrier_semaphore()
    for peer in (partner, across, diagonal):
        pl.semaphore_signal(barrier, inc=1, device_id=(tile, peer), device_id_type=MESH)
    for side in range(4):
        for step in range(PEERS):
            peer = (chan + step) % PEERS
            pl.semaphore_signal(
                barrier, inc=1, device_id=(near[side], peer), device_id_type=MESH
            )

    codes_copy = pltpu.make_async_copy(codes_hbm, codes, codes_sem)
    codes_copy.start()
    x_copies = [
        pltpu.make_async_copy(x_hbm.at[:, pl.ds(q * QW, QW)], g1.at[q, mine, :], x_sem)
        for q in range(Q)
    ]
    for copy in x_copies:
        copy.start()
    w_copies = []
    b_copies = []
    for i, w in enumerate((w0_hbm, w1_hbm, w2_hbm, w3_hbm)):
        w_copies.append(pltpu.make_async_copy(w, w_v.at[i], w_sem.at[i]))
    for i, b in enumerate((b0_hbm, b1_hbm, b2_hbm, b3_hbm)):
        b_copies.append(pltpu.make_async_copy(b, b_v.at[i], b_sem.at[i]))

    lane = iota((1, 128), 1)
    slot = lane // 32
    along = lane % 32

    def wait_bytes(ref, sem):
        pltpu.make_async_copy(ref, ref, sem).wait()

    def pick_tables(code):
        edge = code % 4
        place = jnp.where(code >= 4, S2 - 1 - along, along)
        cell = edge_position(edge, place, S2)
        sel_a[...] = one_hot(iota((S2 * S2, 128), 0) == jnp.where(along < S2, cell, -1))
        corner = 2 * (cell // S2) * S1 + 2 * (cell % S2)
        for part in range(4):
            fine = jnp.where(along < S2, corner + part // 2 * S1 + part % 2, -1)
            sel_enc[:, 128 * part : 128 * part + 128] = one_hot(iota((S1 * S1, 128), 0) == fine)
        place = jnp.where(code >= 4, S1 - 1 - along, along)
        sel_b[...] = one_hot(iota((S2 * S2, 128), 0) == edge_position(edge, place // 2, S2))

    def other_tables():
        row = iota((128, 1), 0)
        for size, exp in ((S1, exp1), (S2, exp2)):
            cell = jnp.where(
                row % 32 < size, edge_position(row // 32, row % 32, size), -1
            )
            exp[...] = one_hot(iota((128, size * size), 1) == cell)
        nxt_enc[...] = dot(exp1[...], sel_enc[...]).astype(BF16)
        nxt_a[...] = dot(exp2[...], sel_a[...]).astype(BF16)
        nxt_b[...] = dot(exp2[...], sel_b[...]).astype(BF16)
        cell = iota((QW, QW), 0)
        pool[...] = one_hot(
            (cell // S1 // 2) * S2 + (cell % S1) // 2 == iota((QW, QW), 1) % (QW // 4)
        )
        cell = iota((1, QW), 1)
        cell = (cell // S1 // 2) * S2 + (cell % S1) // 2
        for q in range(Q):
            up[q] = one_hot(iota((QW, QW), 0) == cell + q * (QW // 4))
        eye = iota((CB, CB), 0) == iota((CB, CB), 1)
        for copy in b_copies:
            copy.wait()
        for i in range(4):
            column = jnp.sum(
                jnp.where(eye, jnp.broadcast_to(b_v[i], (CB, CB)), 0.0), axis=1, keepdims=True
            )
            bias_v[i] = jnp.broadcast_to(column, (CB, 128))

    def pack_rims(layer, picked):
        for side in range(4):
            block = None
            for group in range(4):
                part = picked[16 * group : 16 * group + 16, :]
                shift = (32 * (group - side)) % 128
                if shift:
                    part = pltpu.roll(part, shift, 1)
                block = part if block is None else jnp.where(slot == group, part, block)
            sb[layer, side] = block.astype(BF16)

    def rim_copies(layer):
        copies = []
        for peer in (across, diagonal, partner, chan):
            for side in range(4):
                copies.append(
                    pltpu.make_async_remote_copy(
                        src_ref=sb.at[layer, side],
                        dst_ref=rb.at[layer, chan, side],
                        send_sem=rim_send.at[layer],
                        recv_sem=rim_recv.at[layer],
                        device_id=(near[side], peer),
                        device_id_type=MESH,
                    )
                )
        return copies

    def fine_copies(index, g, source):
        def copies_to(kind, peer, rows, source, recv):
            return [
                pltpu.make_async_remote_copy(
                    src_ref=source(q),
                    dst_ref=g.at[q, rows, :],
                    send_sem=fine_send.at[index, kind],
                    recv_sem=recv[q],
                    device_id=(tile, peer),
                    device_id_type=MESH,
                )
                for q in range(Q)
            ]

        return (
            copies_to(0, partner, mine, source, [partner_recv.at[index]] * Q),
            copies_to(1, across, mine, source, [fine_recv.at[index, 0, q] for q in range(Q)]),
            copies_to(
                2,
                partner,
                across_rows,
                lambda q: g.at[q, across_rows, :],
                [fine_recv.at[index, 1, q] for q in range(Q)],
            ),
        )

    def coarse_copies(index, g):
        def copy_to(peer, rows, recv):
            return pltpu.make_async_remote_copy(
                src_ref=g.at[rows, :],
                dst_ref=g.at[rows, :],
                send_sem=coarse_send.at[index],
                recv_sem=recv,
                device_id=(tile, peer),
                device_id_type=MESH,
            )

        return (
            copy_to(across, mine, across_recv.at[index]),
            copy_to(partner, mine, coarse_recv.at[index]),
            copy_to(partner, across_rows, coarse_recv.at[index]),
        )

    def coarse_start(copies):
        copies[0].start()
        copies[1].start()

    def coarse_relay(copies, index, g):
        copies[0].wait_recv()
        copies[2].start()
        wait_bytes(g.at[pl.ds(0, 2 * CB), :], coarse_recv.at[index])

    def coarse_wait(g, sem):
        wait_bytes(g.at[pl.ds(0, 3 * CB), :], sem)

    def in_two(v):
        high = v.astype(BF16)
        return jnp.concatenate([high, (v - high.astype(F32)).astype(BF16)], axis=0)

    def take(two, table):
        both = dot(two, table)
        return both[:CB] + both[CB:]

    def rim_sums(layer, size):
        blocks = []
        for source in range(PEERS):
            parts = [rb[layer, source, side].astype(F32) for side in range(4)]
            for group in range(4):
                block = None
                for side in range(4):
                    part = parts[side]
                    shift = (32 * (side - group)) % 128
                    if shift:
                        part = pltpu.roll(part, shift, 1)
                    block = part if block is None else jnp.where(slot == side, part, block)
                blocks.append(block.astype(BF16))
        rims = jnp.concatenate(blocks, axis=0)
        r = dot(w_v[layer].reshape(9 * CB, C), rims)
        r = [r[CB * t : CB * t + CB, :] for t in range(9)]

        def by_side(north, south, west, east):
            return jnp.where(
                slot == 0,
                r[north],
                jnp.where(slot == 1, r[south], jnp.where(slot == 2, r[west], r[east])),
            )

        before = jnp.where(along == 0, 0.0, pltpu.roll(by_side(0, 6, 0, 2), 1, 1))
        after = jnp.where(along == size - 1, 0.0, pltpu.roll(by_side(2, 8, 6, 8), 127, 1))
        total = before + by_side(1, 7, 3, 5) + after
        return in_two(total)

    def conv_rows(layer, size, rows):
        cells = size * size
        place = iota((1, cells), 1)
        column = place % size
        sums = []
        for dx in range(3):
            t = [taps[pl.ds(CB * (3 * dy + dx) + rows, 16), :cells] for dy in range(3)]
            above = jnp.where(place >= size, pltpu.roll(t[0], size, 1), 0.0)
            below = jnp.where(place < cells - size, pltpu.roll(t[2], cells - size, 1), 0.0)
            sums.append(t[1] + (above + below))
        left = jnp.where(column == 0, 0.0, pltpu.roll(sums[0], 1, 1))
        right = jnp.where(column == size - 1, 0.0, pltpu.roll(sums[2], cells - 1, 1))
        bias = bias_v[layer, rows : rows + 16, 0:1]
        pre[rows : rows + 16, :cells] = (sums[1] + (left + right)) + bias

    def inner_sums(layer, size):
        for rows in range(0, CB, 16):
            conv_rows(layer, size, rows)

    def activation(size, rows, rims):
        return gelu(pre[rows : rows + 16, : size * size] + rims[rows : rows + 16, :])

    to_partner, to_across, relay = fine_copies(0, g1, lambda q: x_hbm.at[:, pl.ds(q * QW, QW)])
    for copy in b_copies + w_copies:
        copy.start()
    codes_copy.wait()
    codes_here = [codes[side, near[side]] for side in range(4)]
    code = jnp.where(
        slot == 0,
        codes_here[0],
        jnp.where(slot == 1, codes_here[1], jnp.where(slot == 2, codes_here[2], codes_here[3])),
    )
    place = jnp.where(code >= 4, S1 - 1 - along, along)
    cell = edge_position(code % 4, place, S1)
    sel1[...] = one_hot(iota((S1 * S1, 128), 0) == cell)
    wait_bytes(g1.at[:, mine, :], x_sem)
    picked = sum(dot(g1[q, mine, :], sel1[QW * q : QW * q + QW, :]) for q in range(Q))
    pack_rims(0, picked)
    pl.semaphore_wait(barrier, 3 + 4 * PEERS)
    for copy in rim_copies(0):
        copy.start()
    for copy in to_across + to_partner:
        copy.start()
    pick_tables(code)
    other_tables()
    w_copies[0].wait()
    for q in range(Q):
        to_across[q].wait_recv()
        relay[q].start()
    wait_bytes(g1.at[:, mine, :], partner_recv.at[0])
    for q in range(Q):
        relay[q].wait_recv()
        taps[:, QW * q : QW * q + QW] = dot(w_v[0].reshape(9 * CB, C), g1[q])
    inner_sums(0, S1)
    sums = take(in_two(pre[...]), sel_enc[...])
    field = sum(dot(g1[q, mine, :], sel_enc[QW * q : QW * q + QW, :]) for q in range(Q))
    wait_bytes(rb.at[0], rim_recv.at[0])
    two = rim_sums(0, S1)
    edge = (field + gelu(sums + take(two, nxt_enc[...]))).astype(BF16).astype(F32)
    edge = (edge[:, :128] + edge[:, 128:256]) + (edge[:, 256:384] + edge[:, 384:])
    pack_rims(1, edge * 0.25)
    for copy in rim_copies(1):
        copy.start()
    rims = take(two, exp1[...])
    for rows in range(0, CB, 16):
        act = activation(S1, rows, rims)
        own = pl.ds(pl.multiple_of(chan * CB + rows, 16), 16)
        for q in range(Q):
            field = g1[q, own, :].astype(F32)
            g4[q, own, :] = (field + act[:, QW * q : QW * q + QW]).astype(BF16)

    to_partner, to_across, relay = fine_copies(1, g4, lambda q: g4.at[q, mine, :])
    group = iota((1, QW), 1) // (QW // 4)
    pooled = dot(g4[:, mine, :].reshape(Q * CB, QW), pool[...])
    coarse = pooled[:CB]
    for q in range(1, Q):
        coarse = jnp.where(group == q, pooled[CB * q : CB * q + CB], coarse)
    coarse = (coarse * 0.25).astype(BF16)
    middle = coarse
    encoded = sum(dot(g4[q, mine, :], sel1[QW * q : QW * q + QW, :]) for q in range(Q))
    for layer, g in ((1, g2), (2, g3)):
        g[mine, :] = middle
        coarse = coarse_copies(layer - 1, g)
        coarse_start(coarse)
        if layer == 1:
            for copy in to_across + to_partner:
                copy.start()
        else:
            for q in range(Q):
                to_across[q].wait_recv()
                relay[q].start()
        w_copies[layer].wait()
        coarse_relay(coarse, layer - 1, g)
        taps[:, :QW] = dot(w_v[layer].reshape(9 * CB, C), g[...])
        inner_sums(layer, S2)
        sel, nxt = ((sel_a, nxt_a), (sel_b, nxt_b))[layer - 1]
        sums = take(in_two(pre[:, :QW]), sel[...])
        field = dot(middle, sel[...])
        wait_bytes(rb.at[layer], rim_recv.at[layer])
        two = rim_sums(layer, S2)
        edge = (field + gelu(sums + take(two, nxt[...]))).astype(BF16).astype(F32)
        if layer == 2:
            edge = edge + encoded
        pack_rims(layer + 1, edge)
        for copy in rim_copies(layer + 1):
            copy.start()
        rims = take(two, exp2[...])
        parts = []
        for rows in range(0, CB, 16):
            act = activation(S2, rows, rims)
            parts.append((middle[rows : rows + 16, :].astype(F32) + act).astype(BF16))
        middle = jnp.concatenate(parts, axis=0)

    g5[mine, :] = middle
    coarse = coarse_copies(2, g5)
    coarse_start(coarse)
    w_copies[3].wait()
    wait_bytes(g4.at[:, mine, :], partner_recv.at[1])
    for q in range(Q):
        relay[q].wait_recv()
    for index in range(2):
        for kind in range(3):
            wait_bytes(g4.at[:, mine, :], fine_send.at[index, kind])
    for layer in range(3):
        wait_bytes(rb.at[layer], rim_send.at[layer])
    for index in range(2):
        coarse_wait(g2, coarse_send.at[index])
    coarse_relay(coarse, 2, g5)
    for q in range(Q):
        joined[q] = (dot(g5[...], up[q]) + g4[q].astype(F32)).astype(BF16)
        taps[:, QW * q : QW * q + QW] = dot(w_v[3].reshape(9 * CB, C), joined[q])
    inner_sums(3, S1)
    wait_bytes(rb.at[3], rim_send.at[3])
    coarse_wait(g5, coarse_send.at[2])
    wait_bytes(rb.at[3], rim_recv.at[3])
    rims = take(rim_sums(3, S1), exp1[...])
    for rows in range(0, CB, 16):
        act = activation(S1, rows, rims)
        own = pl.ds(pl.multiple_of(chan * CB + rows, 16), 16)
        for q in range(Q):
            field = joined[q, own, :].astype(F32)
            out_ref[rows : rows + 16, QW * q : QW * q + QW] = (
                field + act[:, QW * q : QW * q + QW]
            ).astype(BF16)


def on_device(
    tiles,
    field_in,
    edge_codes,
    weight_enc,
    bias_enc,
    weight_mid_a,
    bias_mid_a,
    weight_mid_b,
    bias_mid_b,
    weight_dec,
    bias_dec,
):
    hbm = pl.BlockSpec(memory_space=pltpu.MemorySpace.HBM)
    vmem = pl.BlockSpec(memory_space=pltpu.MemorySpace.VMEM)
    dma = pltpu.SemaphoreType.DMA
    biases = [b.reshape(1, CB) for b in (bias_enc, bias_mid_a, bias_mid_b, bias_dec)]
    return pl.pallas_call(
        functools.partial(kernel, tiles),
        out_shape=pltpu.MemorySpace.VMEM((CB, S1 * S1), BF16),
        in_specs=[hbm] * 10,
        out_specs=vmem,
        scratch_shapes=[
            pltpu.SMEM((4, tiles), jnp.int32),
            pltpu.VMEM((Q, C, QW), BF16),
            pltpu.VMEM((C, QW), BF16),
            pltpu.VMEM((C, QW), BF16),
            pltpu.VMEM((Q, C, QW), BF16),
            pltpu.VMEM((C, QW), BF16),
            pltpu.VMEM((Q, C, QW), BF16),
            pltpu.VMEM((4, 9, CB, C), BF16),
            pltpu.VMEM((4, 1, CB), F32),
            pltpu.VMEM((4, CB, 128), F32),
            pltpu.VMEM((S1 * S1, 128), BF16),
            pltpu.VMEM((S1 * S1, 4 * 128), BF16),
            pltpu.VMEM((S2 * S2, 128), BF16),
            pltpu.VMEM((S2 * S2, 128), BF16),
            pltpu.VMEM((128, 4 * 128), BF16),
            pltpu.VMEM((128, 128), BF16),
            pltpu.VMEM((128, 128), BF16),
            pltpu.VMEM((128, S1 * S1), BF16),
            pltpu.VMEM((128, S2 * S2), BF16),
            pltpu.VMEM((QW, QW), BF16),
            pltpu.VMEM((Q, QW, QW), BF16),
            pltpu.VMEM((4, 4, 16, 128), BF16),
            pltpu.VMEM((4, PEERS, 4, 16, 128), BF16),
            pltpu.VMEM((9 * CB, S1 * S1), F32),
            pltpu.VMEM((CB, S1 * S1), F32),
            dma,
            dma,
            dma((4,)),
            dma((4,)),
            dma((2, 3)),
            dma((2,)),
            dma((2, 2, Q)),
            dma((3,)),
            dma((3,)),
            dma((3,)),
            dma((4,)),
            dma((4,)),
        ],
        compiler_params=pltpu.CompilerParams(
            collective_id=0, has_side_effects=True, vmem_limit_bytes=62 * 1024 * 1024
        ),
        name="unet_window",
    )(
        edge_codes.T,
        field_in,
        weight_enc,
        weight_mid_a,
        weight_mid_b,
        weight_dec,
        *biases,
    )


def solution(mesh):
    weights = P(None, "chan", None)
    in_specs = (
        P("chan", "face"),
        P(),
        weights,
        P("chan"),
        weights,
        P("chan"),
        weights,
        P("chan"),
        weights,
        P("chan"),
    )
    return jax.shard_map(
        functools.partial(on_device, mesh.shape["face"]),
        mesh=mesh,
        in_specs=in_specs,
        out_specs=P("chan", "face"),
        check_vma=False,
    )
```

```python
import functools

import jax
import jax.numpy as jnp
from jax import lax
from jax.experimental import pallas as pl
from jax.experimental.pallas import tpu as pltpu
from jax.sharding import PartitionSpec as P

TILE_COLS = 4
CB = 64
PEERS = 4
C = CB * PEERS
S1 = 32
S2 = 16
Q = 4
QW = S1 * S1 // Q
GELU_A = 0.7978845608028654
GELU_B = 0.044715
MESH = pl.DeviceIdType.MESH
F32 = jnp.float32
BF16 = jnp.bfloat16


def iota(shape, dim):
    return lax.broadcasted_iota(jnp.int32, shape, dim)


def gelu(v):
    return 0.5 * v * (1.0 + jnp.tanh(GELU_A * (v + GELU_B * (v * v * v))))


def dot(a, b):
    return lax.dot_general(a, b, (((1,), (0,)), ((), ())), preferred_element_type=F32)


def one_hot(cond):
    return jnp.where(cond, 1.0, 0.0).astype(BF16)


def edge_position(edge, along, side):
    return jnp.where(
        edge == 0,
        along,
        jnp.where(
            edge == 1,
            (side - 1) * side + along,
            jnp.where(edge == 2, along * side, along * side + side - 1),
        ),
    )


def kernel(
    tiles,
    codes_hbm,
    x_hbm,
    w0_hbm,
    w1_hbm,
    w2_hbm,
    w3_hbm,
    b0_hbm,
    b1_hbm,
    b2_hbm,
    b3_hbm,
    out_ref,
    codes,
    g1,
    g2,
    g3,
    g4,
    g5,
    joined,
    w_v,
    b_v,
    bias_v,
    sel1,
    sel_enc,
    sel_a,
    sel_b,
    nxt_enc,
    nxt_a,
    nxt_b,
    exp1,
    exp2,
    pool,
    up,
    sb,
    rb,
    taps,
    pre,
    codes_sem,
    x_sem,
    w_sem,
    b_sem,
    fine_send,
    partner_recv,
    fine_recv,
    coarse_send,
    coarse_recv,
    rim_send,
    rim_recv,
):
    tile = lax.axis_index("face")
    chan = lax.axis_index("chan")
    partner = chan + 1 - 2 * (chan % 2)
    across = (chan + 2) % 4
    diagonal = (partner + 2) % 4
    near = [
        (tile + TILE_COLS) % tiles,
        (tile + tiles - TILE_COLS) % tiles,
        (tile + 1) % tiles,
        (tile + tiles - 1) % tiles,
    ]
    mine = pl.ds(pl.multiple_of(chan * CB, CB), CB)
    across_rows = pl.ds(pl.multiple_of(across * CB, CB), CB)

    barrier = pltpu.get_barrier_semaphore()
    for peer in (across, diagonal, partner, chan):
        for side in (3, 2, 1, 0):
            pl.semaphore_signal(
                barrier, inc=1, device_id=(near[side], peer), device_id_type=MESH
            )

    for peer in (partner, across, diagonal):
        pl.semaphore_signal(barrier, inc=1, device_id=(tile, peer), device_id_type=MESH)

    codes_copy = pltpu.make_async_copy(codes_hbm, codes, codes_sem)
    codes_copy.start()
    x_copies = [
        pltpu.make_async_copy(x_hbm.at[:, pl.ds(q * QW, QW)], g1.at[q, mine, :], x_sem)
        for q in range(Q)
    ]
    for copy in x_copies:
        copy.start()
    w_copies = []
    b_copies = []
    for i, w in enumerate((w0_hbm, w1_hbm, w2_hbm, w3_hbm)):
        w_copies.append(pltpu.make_async_copy(w, w_v.at[i], w_sem.at[i]))
    for i, b in enumerate((b0_hbm, b1_hbm, b2_hbm, b3_hbm)):
        b_copies.append(pltpu.make_async_copy(b, b_v.at[i], b_sem.at[i]))

    lane = iota((1, 128), 1)
    slot = lane // 32
    along = lane % 32

    def wait_bytes(ref, sem):
        pltpu.make_async_copy(ref, ref, sem).wait()

    def pick_tables(code):
        edge = code % 4
        place = jnp.where(code >= 4, S2 - 1 - along, along)
        cell = edge_position(edge, place, S2)
        sel_a[...] = one_hot(iota((S2 * S2, 128), 0) == jnp.where(along < S2, cell, -1))
        corner = 2 * (cell // S2) * S1 + 2 * (cell % S2)
        for part in range(4):
            fine = jnp.where(along < S2, corner + part // 2 * S1 + part % 2, -1)
            sel_enc[:, 128 * part : 128 * part + 128] = one_hot(iota((S1 * S1, 128), 0) == fine)
        place = jnp.where(code >= 4, S1 - 1 - along, along)
        sel_b[...] = one_hot(iota((S2 * S2, 128), 0) == edge_position(edge, place // 2, S2))

    def other_tables():
        row = iota((128, 1), 0)
        for size, exp in ((S1, exp1), (S2, exp2)):
            cell = jnp.where(
                row % 32 < size, edge_position(row // 32, row % 32, size), -1
            )
            exp[...] = one_hot(iota((128, size * size), 1) == cell)
        nxt_enc[...] = dot(exp1[...], sel_enc[...]).astype(BF16)
        nxt_a[...] = dot(exp2[...], sel_a[...]).astype(BF16)
        nxt_b[...] = dot(exp2[...], sel_b[...]).astype(BF16)
        cell = iota((QW, QW), 0)
        pool[...] = one_hot(
            (cell // S1 // 2) * S2 + (cell % S1) // 2 == iota((QW, QW), 1) % (QW // 4)
        )
        cell = iota((1, QW), 1)
        cell = (cell // S1 // 2) * S2 + (cell % S1) // 2
        for q in range(Q):
            up[q] = one_hot(iota((QW, QW), 0) == cell + q * (QW // 4))
        eye = iota((CB, CB), 0) == iota((CB, CB), 1)
        for copy in b_copies:
            copy.wait()
        for i in range(4):
            column = jnp.sum(
                jnp.where(eye, jnp.broadcast_to(b_v[i], (CB, CB)), 0.0), axis=1, keepdims=True
            )
            bias_v[i] = jnp.broadcast_to(column, (CB, 128))

    def pack_rims(layer, picked):
        for side in range(4):
            block = None
            for group in range(4):
                part = picked[16 * group : 16 * group + 16, :]
                shift = (32 * (group - side)) % 128
                if shift:
                    part = pltpu.roll(part, shift, 1)
                block = part if block is None else jnp.where(slot == group, part, block)
            sb[layer, side] = block.astype(BF16)

    def rim_copies(layer):
        copies = []
        for peer in (across, diagonal, partner, chan):
            for side in (3, 2, 1, 0):
                copies.append(
                    pltpu.make_async_remote_copy(
                        src_ref=sb.at[layer, side],
                        dst_ref=rb.at[layer, chan, side],
                        send_sem=rim_send.at[layer],
                        recv_sem=rim_recv.at[layer],
                        device_id=(near[side], peer),
                        device_id_type=MESH,
                    )
                )
        return copies

    def fine_copies(index, g, source):
        def copies_to(kind, peer, rows, source, recv):
            return [
                pltpu.make_async_remote_copy(
                    src_ref=source(q),
                    dst_ref=g.at[q, rows, :],
                    send_sem=fine_send.at[index, kind],
                    recv_sem=recv[q],
                    device_id=(tile, peer),
                    device_id_type=MESH,
                )
                for q in range(Q)
            ]

        return (
            copies_to(0, partner, mine, source, [partner_recv.at[index]] * Q),
            copies_to(1, across, mine, source, [fine_recv.at[index, 0, q] for q in range(Q)]),
            copies_to(
                2,
                partner,
                across_rows,
                lambda q: g.at[q, across_rows, :],
                [fine_recv.at[index, 1, q] for q in range(Q)],
            ),
        )

    def coarse_copies(index, g):
        return [
            pltpu.make_async_remote_copy(
                src_ref=g.at[mine, :],
                dst_ref=g.at[mine, :],
                send_sem=coarse_send.at[index],
                recv_sem=coarse_recv.at[index],
                device_id=(tile, peer),
                device_id_type=MESH,
            )
            for peer in (across, diagonal, partner)
        ]

    def coarse_wait(g, sem):
        wait_bytes(g.at[pl.ds(0, 3 * CB), :], sem)

    def in_two(v):
        high = v.astype(BF16)
        return jnp.concatenate([high, (v - high.astype(F32)).astype(BF16)], axis=0)

    def take(two, table):
        both = dot(two, table)
        return both[:CB] + both[CB:]

    def rim_sums(layer, size):
        blocks = []
        for source in range(PEERS):
            parts = [rb[layer, source, side].astype(F32) for side in range(4)]
            for group in range(4):
                block = None
                for side in range(4):
                    part = parts[side]
                    shift = (32 * (side - group)) % 128
                    if shift:
                        part = pltpu.roll(part, shift, 1)
                    block = part if block is None else jnp.where(slot == side, part, block)
                blocks.append(block.astype(BF16))
        rims = jnp.concatenate(blocks, axis=0)
        r = dot(w_v[layer].reshape(9 * CB, C), rims)
        r = [r[CB * t : CB * t + CB, :] for t in range(9)]

        def by_side(north, south, west, east):
            return jnp.where(
                slot == 0,
                r[north],
                jnp.where(slot == 1, r[south], jnp.where(slot == 2, r[west], r[east])),
            )

        before = jnp.where(along == 0, 0.0, pltpu.roll(by_side(0, 6, 0, 2), 1, 1))
        after = jnp.where(along == size - 1, 0.0, pltpu.roll(by_side(2, 8, 6, 8), 127, 1))
        total = before + by_side(1, 7, 3, 5) + after
        return in_two(total)

    def conv_rows(layer, size, rows):
        cells = size * size
        place = iota((1, cells), 1)
        column = place % size
        sums = []
        for dx in range(3):
            t = [taps[pl.ds(CB * (3 * dy + dx) + rows, 16), :cells] for dy in range(3)]
            above = jnp.where(place >= size, pltpu.roll(t[0], size, 1), 0.0)
            below = jnp.where(place < cells - size, pltpu.roll(t[2], cells - size, 1), 0.0)
            sums.append(t[1] + (above + below))
        left = jnp.where(column == 0, 0.0, pltpu.roll(sums[0], 1, 1))
        right = jnp.where(column == size - 1, 0.0, pltpu.roll(sums[2], cells - 1, 1))
        bias = bias_v[layer, rows : rows + 16, 0:1]
        pre[rows : rows + 16, :cells] = (sums[1] + (left + right)) + bias

    def inner_sums(layer, size):
        for rows in range(0, CB, 16):
            conv_rows(layer, size, rows)

    def activation(size, rows, rims):
        return gelu(pre[rows : rows + 16, : size * size] + rims[rows : rows + 16, :])

    to_partner, to_across, relay = fine_copies(0, g1, lambda q: x_hbm.at[:, pl.ds(q * QW, QW)])
    for copy in b_copies + w_copies:
        copy.start()
    codes_copy.wait()
    codes_here = [codes[side, near[side]] for side in range(4)]
    code = jnp.where(
        slot == 0,
        codes_here[0],
        jnp.where(slot == 1, codes_here[1], jnp.where(slot == 2, codes_here[2], codes_here[3])),
    )
    place = jnp.where(code >= 4, S1 - 1 - along, along)
    cell = edge_position(code % 4, place, S1)
    sel1[...] = one_hot(iota((S1 * S1, 128), 0) == cell)
    wait_bytes(g1.at[:, mine, :], x_sem)
    picked = sum(dot(g1[q, mine, :], sel1[QW * q : QW * q + QW, :]) for q in range(Q))
    pack_rims(0, picked)
    pl.semaphore_wait(barrier, 3 + 4 * PEERS)
    for copy in rim_copies(0):
        copy.start()
    for copy in to_across + to_partner:
        copy.start()
    pick_tables(code)
    other_tables()
    w_copies[0].wait()
    for q in range(Q):
        to_across[q].wait_recv()
        relay[q].start()
    wait_bytes(g1.at[:, mine, :], partner_recv.at[0])
    for q in range(Q):
        relay[q].wait_recv()
        taps[:, QW * q : QW * q + QW] = dot(w_v[0].reshape(9 * CB, C), g1[q])
    inner_sums(0, S1)
    sums = take(in_two(pre[...]), sel_enc[...])
    field = sum(dot(g1[q, mine, :], sel_enc[QW * q : QW * q + QW, :]) for q in range(Q))
    wait_bytes(rb.at[0], rim_recv.at[0])
    two = rim_sums(0, S1)
    edge = (field + gelu(sums + take(two, nxt_enc[...]))).astype(BF16).astype(F32)
    edge = (edge[:, :128] + edge[:, 128:256]) + (edge[:, 256:384] + edge[:, 384:])
    pack_rims(1, edge * 0.25)
    for copy in rim_copies(1):
        copy.start()
    rims = take(two, exp1[...])
    for rows in range(0, CB, 16):
        act = activation(S1, rows, rims)
        own = pl.ds(pl.multiple_of(chan * CB + rows, 16), 16)
        for q in range(Q):
            field = g1[q, own, :].astype(F32)
            g4[q, own, :] = (field + act[:, QW * q : QW * q + QW]).astype(BF16)

    to_partner, to_across, relay = fine_copies(1, g4, lambda q: g4.at[q, mine, :])
    group = iota((1, QW), 1) // (QW // 4)
    pooled = dot(g4[:, mine, :].reshape(Q * CB, QW), pool[...])
    coarse = pooled[:CB]
    for q in range(1, Q):
        coarse = jnp.where(group == q, pooled[CB * q : CB * q + CB], coarse)
    coarse = (coarse * 0.25).astype(BF16)
    middle = coarse
    encoded = sum(dot(g4[q, mine, :], sel1[QW * q : QW * q + QW, :]) for q in range(Q))
    for layer, g in ((1, g2), (2, g3)):
        g[mine, :] = middle
        for copy in coarse_copies(layer - 1, g):
            copy.start()
        if layer == 1:
            for copy in to_across + to_partner:
                copy.start()
        else:
            for q in range(Q):
                to_across[q].wait_recv()
                relay[q].start()
        w_copies[layer].wait()
        coarse_wait(g, coarse_recv.at[layer - 1])
        taps[:, :QW] = dot(w_v[layer].reshape(9 * CB, C), g[...])
        inner_sums(layer, S2)
        sel, nxt = ((sel_a, nxt_a), (sel_b, nxt_b))[layer - 1]
        sums = take(in_two(pre[:, :QW]), sel[...])
        field = dot(middle, sel[...])
        wait_bytes(rb.at[layer], rim_recv.at[layer])
        two = rim_sums(layer, S2)
        edge = (field + gelu(sums + take(two, nxt[...]))).astype(BF16).astype(F32)
        if layer == 2:
            edge = edge + encoded
        pack_rims(layer + 1, edge)
        for copy in rim_copies(layer + 1):
            copy.start()
        rims = take(two, exp2[...])
        parts = []
        for rows in range(0, CB, 16):
            act = activation(S2, rows, rims)
            parts.append((middle[rows : rows + 16, :].astype(F32) + act).astype(BF16))
        middle = jnp.concatenate(parts, axis=0)

    g5[mine, :] = middle
    for copy in coarse_copies(2, g5):
        copy.start()
    w_copies[3].wait()
    wait_bytes(g4.at[:, mine, :], partner_recv.at[1])
    for q in range(Q):
        relay[q].wait_recv()
    for index in range(2):
        for kind in range(3):
            wait_bytes(g4.at[:, mine, :], fine_send.at[index, kind])
    for layer in range(3):
        wait_bytes(rb.at[layer], rim_send.at[layer])
    for index in range(2):
        coarse_wait(g2, coarse_send.at[index])
    coarse_wait(g5, coarse_recv.at[2])
    for q in range(Q):
        joined[q] = (dot(g5[...], up[q]) + g4[q].astype(F32)).astype(BF16)
        taps[:, QW * q : QW * q + QW] = dot(w_v[3].reshape(9 * CB, C), joined[q])
    inner_sums(3, S1)
    wait_bytes(rb.at[3], rim_send.at[3])
    coarse_wait(g5, coarse_send.at[2])
    wait_bytes(rb.at[3], rim_recv.at[3])
    rims = take(rim_sums(3, S1), exp1[...])
    for rows in range(0, CB, 16):
        act = activation(S1, rows, rims)
        own = pl.ds(pl.multiple_of(chan * CB + rows, 16), 16)
        for q in range(Q):
            field = joined[q, own, :].astype(F32)
            out_ref[rows : rows + 16, QW * q : QW * q + QW] = (
                field + act[:, QW * q : QW * q + QW]
            ).astype(BF16)


def on_device(
    tiles,
    field_in,
    edge_codes,
    weight_enc,
    bias_enc,
    weight_mid_a,
    bias_mid_a,
    weight_mid_b,
    bias_mid_b,
    weight_dec,
    bias_dec,
):
    hbm = pl.BlockSpec(memory_space=pltpu.MemorySpace.HBM)
    vmem = pl.BlockSpec(memory_space=pltpu.MemorySpace.VMEM)
    dma = pltpu.SemaphoreType.DMA
    biases = [b.reshape(1, CB) for b in (bias_enc, bias_mid_a, bias_mid_b, bias_dec)]
    return pl.pallas_call(
        functools.partial(kernel, tiles),
        out_shape=pltpu.MemorySpace.VMEM((CB, S1 * S1), BF16),
        in_specs=[hbm] * 10,
        out_specs=vmem,
        scratch_shapes=[
            pltpu.SMEM((4, tiles), jnp.int32),
            pltpu.VMEM((Q, C, QW), BF16),
            pltpu.VMEM((C, QW), BF16),
            pltpu.VMEM((C, QW), BF16),
            pltpu.VMEM((Q, C, QW), BF16),
            pltpu.VMEM((C, QW), BF16),
            pltpu.VMEM((Q, C, QW), BF16),
            pltpu.VMEM((4, 9, CB, C), BF16),
            pltpu.VMEM((4, 1, CB), F32),
            pltpu.VMEM((4, CB, 128), F32),
            pltpu.VMEM((S1 * S1, 128), BF16),
            pltpu.VMEM((S1 * S1, 4 * 128), BF16),
            pltpu.VMEM((S2 * S2, 128), BF16),
            pltpu.VMEM((S2 * S2, 128), BF16),
            pltpu.VMEM((128, 4 * 128), BF16),
            pltpu.VMEM((128, 128), BF16),
            pltpu.VMEM((128, 128), BF16),
            pltpu.VMEM((128, S1 * S1), BF16),
            pltpu.VMEM((128, S2 * S2), BF16),
            pltpu.VMEM((QW, QW), BF16),
            pltpu.VMEM((Q, QW, QW), BF16),
            pltpu.VMEM((4, 4, 16, 128), BF16),
            pltpu.VMEM((4, PEERS, 4, 16, 128), BF16),
            pltpu.VMEM((9 * CB, S1 * S1), F32),
            pltpu.VMEM((CB, S1 * S1), F32),
            dma,
            dma,
            dma((4,)),
            dma((4,)),
            dma((2, 3)),
            dma((2,)),
            dma((2, 2, Q)),
            dma((3,)),
            dma((3,)),
            dma((4,)),
            dma((4,)),
        ],
        compiler_params=pltpu.CompilerParams(
            collective_id=0, has_side_effects=True, vmem_limit_bytes=62 * 1024 * 1024
        ),
        name="unet_window",
    )(
        edge_codes.T,
        field_in,
        weight_enc,
        weight_mid_a,
        weight_mid_b,
        weight_dec,
        *biases,
    )


def solution(mesh):
    weights = P(None, "chan", None)
    in_specs = (
        P("chan", "face"),
        P(),
        weights,
        P("chan"),
        weights,
        P("chan"),
        weights,
        P("chan"),
        weights,
        P("chan"),
    )
    return jax.shard_map(
        functools.partial(on_device, mesh.shape["face"]),
        mesh=mesh,
        in_specs=in_specs,
        out_specs=P("chan", "face"),
        check_vma=False,
    )
```
